32 devices in a mesh: dp: 4 (over y, x), row: 2 (over core), col: 4 (over z).
Axes of the slice: x: 2, y: 2, z: 4, core: 2. Of those that a mesh axis runs over, the one named last changes fastest.
Arguments:
- features: bfloat16 [4, 40, 160, 640], P('dp', 'row', 'col'), may hold values from -800 to 800
- hole_mask: int32 [4, 40, 160], P('dp', 'row', 'col'), may hold values 0 or 1
- norm_gain: float32 [640], replicated, may hold values from 0.5 to 1.5
- norm_shift: float32 [640], replicated, may hold values from -3 to 3
- conv_weight: bfloat16 [9, 640, 640], P(None, 'dp'), may hold values from -0.078125 to 0.078125
- mask_weight: float32 [9, 640], replicated, may hold values from -3 to 3
- conv_bias: float32 [640], replicated, may hold values from -3 to 3
Outputs:
- conv_out: bfloat16 [4, 40, 160, 640], P('dp', 'row', 'col')
The draws below stay inside these ranges and needn't reach their ends.
All inputs are finite; a program needn't handle non-finite values. No bound on the sum of `hole_mask` on one device may be relied on, other than what follows from the above.
Results may differ from the reference program's by a relative error of at most 0.0032.
Values may be sent and summed in bfloat16 or wider, within the bound.
No kernel may reach another device: no remote copies, remote signals or barrier semaphores. Data moves between devices by JAX's collectives and lax.ppermute only.
A program may use at most 128 MiB of HBM per device.

```python
import jax
import jax.numpy as jnp
from jax import lax

CH = 640
GROUPS = 32
ROWS_DEV = 20
COLS_DEV = 40
IMG_H = 40
IMG_W = 160
BATCH = 4


def draw_features(key, part):
    key_base, key_chan, key_offset, key_tile = jax.random.split(key, 4)
    shape = (BATCH, IMG_H, IMG_W, CH)
    rows = jnp.arange(IMG_H, dtype=jnp.float32) / max(IMG_H - 1, 1)
    cols = jnp.arange(IMG_W, dtype=jnp.float32) / max(IMG_W - 1, 1)
    ramp = jnp.power(3.0, rows - 0.5)[:, None] * jnp.power(3.0, cols - 0.5)[None, :]
    tile_rows = max(ROWS_DEV // 2, 1)
    tile_cols = max(COLS_DEV // 4, 1)
    row_tiles = (IMG_H + tile_rows - 1) // tile_rows
    col_tiles = (IMG_W + tile_cols - 1) // tile_cols
    tile_power = jax.random.uniform(key_tile, (BATCH, row_tiles, col_tiles), jnp.float32, -1.0, 1.0)
    tile_gain = jnp.power(3.0, tile_power)
    row_index = jnp.arange(IMG_H) // tile_rows
    col_index = jnp.arange(IMG_W) // tile_cols
    spatial = tile_gain[:, row_index[:, None], col_index[None, :]] * ramp[None, :, :]
    base = jax.random.truncated_normal(key_base, -4.0, 4.0, shape, jnp.float32)
    offset = jax.random.uniform(key_offset, (BATCH, 1, 1, CH), jnp.float32, -1.0, 1.0)
    chan = jnp.power(10.0, jax.random.uniform(key_chan, (CH,), jnp.float32, 0.0, 1.0))
    return ((base + offset) * spatial[:, :, :, None] * chan).astype(jnp.bfloat16)


def with_ends(values, own_key, least, largest):
    longest = values.shape.index(max(values.shape))
    spots = []
    for shift in (0, 1):
        where = [jax.random.randint(jax.random.fold_in(own_key, axis), (), 0, length) for axis, length in enumerate(values.shape)]
        where[longest] = (where[longest] + shift) % values.shape[longest]
        spots.append(tuple(where))
    return values.at[spots[0]].set(least).at[spots[1]].set(largest)


def levels(key, dims, pieces, low, top_value):
    factor_of, own = 1.0, jax.random.fold_in(key, 6)
    for dim, shards_of in pieces:
        heights = jnp.exp(jax.random.uniform(jax.random.fold_in(own, dim), (shards_of,), jnp.float32, low / len(pieces), top_value / len(pieces)))
        factor_of = factor_of * jnp.repeat(heights, dims[dim] // shards_of).reshape([-1 if axis == dim else 1 for axis in range(len(dims))])
    return factor_of


def scatter_about(own_key, dims, width, bound, cuts=(), kind=jnp.bfloat16):
    loudness = levels(own_key, dims, cuts, -0.22, 0.18) if cuts else 1.0
    drawn = jax.random.normal(own_key, dims, jnp.float32) * width * loudness
    return jnp.minimum(jnp.maximum(drawn, -bound), bound).astype(kind)


def setup_inputs(seed: int = 0) -> dict:
    key_list = jax.random.split(jax.random.key(seed), 8)
    return {
        "features": draw_features(jax.random.fold_in(key_list[7], 71), 0),
        "hole_mask": with_ends((jax.random.randint(key_list[1], (BATCH, IMG_H, IMG_W), 0, 2) < 1).astype(jnp.int32), jax.random.fold_in(key_list[1], 1), 0, 1),
        "norm_gain": jnp.clip(jax.random.uniform(key_list[2], (CH,), jnp.float32, 0.5, 1.5), 0.5, 1.5),
        "norm_shift": scatter_about(key_list[3], (CH,), 0.5, 3.0, (), jnp.float32),
        "conv_weight": scatter_about(key_list[4], (9, CH, CH), (9 * CH) ** -0.5, 0.078125, ((1, 4),)),
        "mask_weight": scatter_about(key_list[5], (9, CH), 0.5, 3.0, (), jnp.float32),
        "conv_bias": scatter_about(key_list[6], (CH,), 0.5, 3.0, (), jnp.float32),
    }


EPS = 1e-05

def reference(features, hole_mask, norm_gain, norm_shift, conv_weight, mask_weight, conv_bias):
    weight_full = conv_weight.astype(jnp.float32)

    def one_image(pair):
        image, holes = pair
        grouped = image.astype(jnp.float32).reshape(IMG_H, IMG_W, GROUPS, CH // GROUPS)
        mean_val = lax.optimization_barrier(jnp.mean(grouped, axis=(0, 1, 3)))
        deviate = grouped - mean_val[None, None, :, None]
        var_val = lax.optimization_barrier(jnp.mean(deviate * deviate, axis=(0, 1, 3)))
        normed = (deviate * lax.rsqrt(var_val + EPS)[None, None, :, None]).reshape(IMG_H, IMG_W, CH)
        act_low = jax.nn.silu(normed * norm_gain + norm_shift).astype(jnp.bfloat16)
        act_full = lax.optimization_barrier(act_low).astype(jnp.float32)
        padded = jnp.pad(act_full, ((1, 1), (1, 1), (0, 0)))
        mask_pad = jnp.pad(holes.astype(jnp.float32), 1)
        total = jnp.zeros((IMG_H, IMG_W, CH), jnp.float32) + conv_bias
        for tap in range(9):
            row_off = tap // 3
            col_off = tap % 3
            window = padded[row_off:row_off + IMG_H, col_off:col_off + IMG_W].reshape(IMG_H * IMG_W, CH)
            prod = jnp.dot(window, weight_full[tap], precision=lax.Precision.HIGHEST, preferred_element_type=jnp.float32)
            total = total + prod.reshape(IMG_H, IMG_W, CH)
            total = total + mask_pad[row_off:row_off + IMG_H, col_off:col_off + IMG_W, None] * mask_weight[tap]
        return total.astype(jnp.bfloat16)
    return lax.map(one_image, (features, hole_mask))
```

```python
import functools

import jax
import jax.numpy as jnp
from jax import lax
from jax.experimental import pallas as pl
from jax.experimental.pallas import tpu as pltpu
from jax.sharding import PartitionSpec as P

GROUPS = 32
EPS = 1e-05
TAPS = 9
PARTS = 4


VMEM = pl.BlockSpec(memory_space=pltpu.VMEM)
SMEM = pl.BlockSpec(memory_space=pltpu.SMEM)


def swap(value, axis, bit):
    size = lax.axis_size(axis)
    return lax.ppermute(value, axis, [(i, i ^ bit) for i in range(size)])


def shift(value, axis, step):
    size = lax.axis_size(axis)
    pairs = [(i, i + step) for i in range(size) if 0 <= i + step < size]
    return lax.ppermute(value, axis, pairs)


def after(value, *others):
    return lax.optimization_barrier((value, *others))[0]


def segments(half, depth, rows):
    pieces = []
    at = half * rows
    while at < (half + 1) * rows:
        tap, first = divmod(at, depth)
        width = min(depth - first, (half + 1) * rows - at)
        pieces.append((tap, first, width))
        at += width
    return pieces


def windows_kernel(rows, cols, depth, half_rows, flags, cells, left, right, mean, gain, offset, out, even, odd, kept):
    channels = cells.shape[-1]
    padded_rows = out.shape[-1]
    group = 2 * cols
    mean_row, gain_row, offset_row = mean[...], gain[...], offset[...]

    def act(x):
        v = (x.astype(jnp.float32) - mean_row) * gain_row + offset_row
        return v / (1.0 + jnp.exp(-v))

    left_act = act(left[...]) * flags[2]
    right_act = act(right[...]) * flags[3]
    place = lax.broadcasted_iota(jnp.int32, (cols, channels), 0)

    def row_of(r):
        value = act(cells[r])
        lo, hi = left_act[r : r + 1], right_act[r : r + 1]
        if r == 0 or r == rows + 1:
            keep = flags[0] if r == 0 else flags[1]
            value, lo, hi = value * keep, lo * keep, hi * keep
        before = jnp.where(place == 0, jnp.broadcast_to(lo, value.shape), pltpu.roll(value, 1, 0))
        behind = jnp.where(
            place == cols - 1, jnp.broadcast_to(hi, value.shape), pltpu.roll(value, cols - 1, 0)
        )
        return before, value, behind

    for pair in range(rows // 2 + 1):
        one = row_of(2 * pair)
        two = row_of(2 * pair + 1)
        for dx in range(3):
            even[dx, pair * group : (pair + 1) * group, :] = jnp.concatenate(
                [one[dx], two[dx]], axis=0
            ).astype(jnp.bfloat16)
            if pair:
                odd[dx, (pair - 1) * group : pair * group, :] = jnp.concatenate(
                    [kept[dx], one[dx]], axis=0
                ).astype(jnp.bfloat16)
            kept[dx] = two[dx]

    def fill(step, carry):
        at = pl.multiple_of(step * group, group)
        for part in range(PARTS):
            for half in range(2):
                pieces = []
                for tap, first, width in segments(half, depth, half_rows):
                    source = odd if tap // 3 == 1 else even
                    start = at + (group if tap // 3 == 2 else 0)
                    lane = part * depth + first
                    pieces.append(source[tap % 3, pl.ds(start, group), lane : lane + width])
                if padded_rows > half_rows:
                    pieces.append(jnp.zeros((group, padded_rows - half_rows), jnp.bfloat16))
                out[2 * part + half, pl.ds(at, group), :] = jnp.concatenate(pieces, axis=1)
        return carry

    lax.fori_loop(0, rows // 2, fill, 0)


def first_kernel(half_rows, spots, lhs, weight, masks, rows_of_mask, out, held):
    pad = held.shape[0] - half_rows
    table = rows_of_mask[...]
    high = table.astype(jnp.bfloat16)
    rest = table - high.astype(jnp.float32)
    middle = rest.astype(jnp.bfloat16)
    low = (rest - middle.astype(jnp.float32)).astype(jnp.bfloat16)
    total = None
    for piece in (high, middle, low):
        term = lax.dot_general(
            masks[...], piece, (((0,), (0,)), ((), ())), preferred_element_type=jnp.float32
        )
        total = term if total is None else total + term
    if pad:
        held[half_rows:, :] = jnp.zeros((pad, held.shape[1]), held.dtype)
    for half in range(2):
        held[:half_rows, :] = weight[half * half_rows : (half + 1) * half_rows, :]
        total = total + jnp.dot(lhs[spots[half]], held[...], preferred_element_type=jnp.float32)
    out[...] = total


def next_kernel(half_rows, spots, lhs, one, two, three, four, total, out, held):
    pad = held.shape[0] - half_rows
    cut = one.shape[0]
    if pad:
        held[half_rows:, :] = jnp.zeros((pad, held.shape[1]), held.dtype)
    result = total[...]
    for spot, (head, tail) in enumerate(((one, two), (three, four))):
        held[:cut, :] = head[...]
        held[cut:half_rows, :] = tail[...]
        result = result + jnp.dot(lhs[spots[spot]], held[...], preferred_element_type=jnp.float32)
    out[...] = result.astype(out.dtype)


def params(mib):
    return pltpu.CompilerParams(vmem_limit_bytes=mib << 20)


def local(features, hole_mask, norm_gain, norm_shift, conv_weight, mask_weight, conv_bias):
    rows, cols, channels = features.shape[1:]
    cells = rows * cols
    per_group = channels // GROUPS
    n_dp, n_row, n_col = lax.axis_size("dp"), lax.axis_size("row"), lax.axis_size("col")
    stride = n_dp // PARTS
    at_dp, at_row, at_col = lax.axis_index("dp"), lax.axis_index("row"), lax.axis_index("col")
    half = at_row % 2

    shard = conv_weight
    bit = 1
    while bit < stride:
        other = swap(shard, "dp", bit)
        upper = (at_dp // bit) % 2 == 1
        shard = jnp.concatenate(
            [jnp.where(upper, other, shard), jnp.where(upper, shard, other)], axis=1
        )
        bit *= 2
    depth = shard.shape[1]
    part = at_dp // stride
    weight = shard.reshape(TAPS * depth, channels)
    half_rows = TAPS * depth // 2
    padded_rows = -(-half_rows // 256) * 256
    cut = -(-(half_rows // 2) // 128) * 128

    piece_a = lax.dynamic_slice_in_dim(weight, half * half_rows, cut, axis=0)
    piece_b = lax.dynamic_slice_in_dim(weight, half * half_rows + cut, half_rows - cut, axis=0)

    image = features[0]
    mask = hole_mask[0].astype(jnp.bfloat16)

    x_b = swap(piece_b, "dp", stride)
    y_a = swap(piece_a, "dp", 2 * stride)

    def row_message(r):
        extra = jnp.pad(mask[r : r + 1], ((0, 0), (0, channels - cols)))
        return jnp.concatenate([image[r], extra], axis=0)

    if n_row == 2:
        got = swap(jnp.where(at_row == 0, row_message(rows - 1), row_message(0)), "row", 1)
        above = below = got
    else:
        above = shift(row_message(rows - 1), "row", 1)
        below = shift(row_message(0), "row", -1)
    top = (at_row > 0).astype(jnp.float32)
    bottom = (at_row < n_row - 1).astype(jnp.float32)
    leftmost = (at_col > 0).astype(jnp.float32)
    rightmost = (at_col < n_col - 1).astype(jnp.float32)

    grouped = image.astype(jnp.float32)
    sums = jnp.sum(grouped, axis=(0, 1)).reshape(GROUPS, per_group).sum(axis=1)
    count = float(cells * per_group)
    mean = sums / count
    deviate = grouped - jnp.repeat(mean, per_group)
    spread = jnp.sum(deviate * deviate, axis=(0, 1)).reshape(GROUPS, per_group).sum(axis=1)
    stats = jnp.stack([mean, spread])
    for axis, size in (("row", n_row), ("col", n_col)):
        bit = 1
        while bit < size:
            other = swap(stats, axis, bit)
            gap = stats[0] - other[0]
            stats = jnp.stack(
                [
                    (stats[0] + other[0]) * 0.5,
                    stats[1] + other[1] + gap * gap * (count * 0.5),
                ]
            )
            count *= 2.0
            bit *= 2

    def bordered(mask_above, mask_below):
        return jnp.concatenate([mask_above, mask, mask_below], axis=0)

    mask_rows = bordered(
        above[cols:, :cols] * top.astype(jnp.bfloat16),
        below[cols:, :cols] * bottom.astype(jnp.bfloat16),
    )
    tall = jnp.concatenate([above[None, :cols], image, below[None, :cols]], axis=0)

    def col_message(c):
        return jnp.concatenate(
            [tall[:, c], jnp.pad(mask_rows[:, c : c + 1], ((0, 0), (0, 127)))], axis=1
        )

    left = shift(col_message(cols - 1), "col", 1)
    right = shift(col_message(0), "col", -1)

    x_a = swap(piece_a, "dp", stride)
    y_b = swap(piece_b, "dp", 2 * stride)
    d_a = swap(y_a, "dp", stride)
    d_b = swap(x_b, "dp", 2 * stride)

    wide = jnp.concatenate(
        [left[:, channels : channels + 1], mask_rows, right[:, channels : channels + 1]], axis=1
    )
    masks = jnp.stack(
        [wide[t // 3 : t // 3 + rows, t % 3 : t % 3 + cols] for t in range(TAPS)]
    ).reshape(TAPS, cells)
    masks = jnp.concatenate(
        [masks, jnp.ones((1, cells), jnp.bfloat16), jnp.zeros((6, cells), jnp.bfloat16)], axis=0
    )
    table = jnp.concatenate(
        [mask_weight, conv_bias[None], jnp.zeros((6, channels), jnp.float32)], axis=0
    )

    inverse = lax.rsqrt(stats[1] / count + EPS)
    gain = (jnp.repeat(inverse, per_group) * norm_gain)[None]
    mean_row = jnp.repeat(stats[0], per_group)[None]
    flags = jnp.stack([top, bottom, leftmost, rightmost])
    lhs = pl.pallas_call(
        functools.partial(windows_kernel, rows, cols, depth, half_rows),
        out_shape=jax.ShapeDtypeStruct((2 * PARTS, cells, padded_rows), jnp.bfloat16),
        in_specs=[SMEM] + [VMEM] * 6,
        out_specs=VMEM,
        scratch_shapes=[
            pltpu.VMEM((3, cells + 2 * cols, channels), jnp.bfloat16),
            pltpu.VMEM((3, cells, channels), jnp.bfloat16),
            pltpu.VMEM((3, cols, channels), jnp.float32),
        ],
        compiler_params=params(12),
        cost_estimate=pl.CostEstimate(flops=0, bytes_accessed=12 << 20, transcendentals=0),
        name="windows",
    )(flags, tall, left[:, :channels], right[:, :channels], mean_row, gain, norm_shift[None])

    held = pltpu.VMEM((padded_rows, channels), jnp.bfloat16)
    flops = 4 * cells * half_rows * channels
    cost = pl.CostEstimate(flops=flops, bytes_accessed=4 << 20, transcendentals=0)
    total = pl.pallas_call(
        functools.partial(first_kernel, half_rows),
        out_shape=jax.ShapeDtypeStruct((cells, channels), jnp.float32),
        in_specs=[SMEM] + [VMEM] * 4,
        out_specs=VMEM,
        scratch_shapes=[held],
        compiler_params=params(8),
        cost_estimate=cost,
        name="first",
    )(jnp.stack([2 * part, 2 * part + 1]), lhs, weight, masks, table)

    for number, (head, tail) in enumerate(((x_a, x_b), (y_a, y_b), (d_a, d_b))):
        owner = part ^ (number + 1)
        spots = jnp.stack([2 * owner + half, 2 * owner + 1 - half])
        last = number == 2
        total = pl.pallas_call(
            functools.partial(next_kernel, half_rows),
            out_shape=jax.ShapeDtypeStruct(
                (cells, channels), jnp.bfloat16 if last else jnp.float32
            ),
            in_specs=[SMEM] + [VMEM] * 6,
            out_specs=VMEM,
            scratch_shapes=[held],
            compiler_params=params(8),
            cost_estimate=cost,
            name="last" if last else "next",
        )(spots, lhs, head, tail, swap(head, "row", 1), swap(tail, "row", 1), total)
    return total.reshape(1, rows, cols, channels)


def solution(mesh):
    in_specs = (
        P("dp", "row", "col", None),
        P("dp", "row", "col"),
        P(),
        P(),
        P(None, "dp", None),
        P(),
        P(),
    )
    out_specs = P("dp", "row", "col", None)
    return jax.shard_map(local, mesh=mesh, in_specs=in_specs, out_specs=out_specs, check_vma=False)
```

```python
import functools

import jax
import jax.numpy as jnp
from jax import lax
from jax.experimental import pallas as pl
from jax.experimental.pallas import tpu as pltpu
from jax.sharding import PartitionSpec as P


GROUPS = 32
EPS = 1e-05
TAPS = 9
PARTS = 4
LANES = 128


VMEM = pl.BlockSpec(memory_space=pltpu.VMEM)
HBM = pl.BlockSpec(memory_space=pltpu.HBM)
F32 = jnp.float32
BF16 = jnp.bfloat16


def swap(value, axis, bit):
    size = lax.axis_size(axis)
    return lax.ppermute(value, axis, [(i, i ^ bit) for i in range(size)])


def shift(value, axis, step):
    size = lax.axis_size(axis)
    pairs = [(i, i + step) for i in range(size) if 0 <= i + step < size]
    return lax.ppermute(value, axis, pairs)


def after(value, *others):
    return lax.optimization_barrier((value, *others))[0]


def params(mib):
    return pltpu.CompilerParams(vmem_limit_bytes=mib << 20)


def cost(flops, size):
    return pl.CostEstimate(flops=flops, bytes_accessed=size, transcendentals=0)


def thirds(value):
    high = value.astype(BF16)
    rest = value - high.astype(F32)
    middle = rest.astype(BF16)
    low = (rest - middle.astype(F32)).astype(BF16)
    return high, middle, low


def exact_dot(value, ones, dims):
    total = None
    for piece in thirds(value):
        term = lax.dot_general(piece, ones, (dims, ((), ())), preferred_element_type=F32)
        total = term if total is None else total + term
    return total


def by_group(value, member):
    return exact_dot(jnp.broadcast_to(value, (16, value.shape[1])), member, ((1,), (0,)))[:1]


def by_channel(value, member):
    return exact_dot(jnp.broadcast_to(value, (16, value.shape[1])), member, ((1,), (1,)))[:1]


def merged(mean, spread, other_mean, other_spread, count):
    gap = mean - other_mean
    return (mean + other_mean) * 0.5, spread + other_spread + gap * gap * (count * 0.5)


def edges_kept(count_row, count_col):
    row, col = lax.axis_index("row"), lax.axis_index("col")
    inside = (row > 0, row < count_row - 1, col > 0, col < count_col - 1)
    return [jnp.where(flag, 1.0, 0.0).astype(F32) for flag in inside]


def even_col():
    return lax.rem(lax.axis_index("col"), 2) == 0


def segments(half, depth, rows):
    pieces = []
    at = half * rows
    while at < (half + 1) * rows:
        tap, first = divmod(at, depth)
        width = min(depth - first, (half + 1) * rows - at)
        pieces.append((tap, first, width))
        at += width
    return pieces


def cut_kernel(weight, head, tail, sems):
    rows, first = head.shape[0] + tail.shape[0], head.shape[0]
    at = pl.multiple_of(lax.rem(lax.axis_index("row"), 2) * rows, 16)
    one = pltpu.make_async_copy(weight.at[pl.ds(at, first)], head, sems.at[0])
    two = pltpu.make_async_copy(
        weight.at[pl.ds(pl.multiple_of(at + first, 16), rows - first)], tail, sems.at[1]
    )
    one.start()
    two.start()
    one.wait()
    two.wait()


def stats_kernel(per_group, cells, mask, member, up, down, stats):
    rows, cols, channels = cells.shape
    count = float(rows * cols)
    total = jnp.zeros((cols, channels), F32)
    for r in range(rows):
        total = total + cells[r].astype(F32)
    sums = jnp.sum(total, axis=0, keepdims=True)
    mean = by_group(sums, member[...]) * (1.0 / (count * per_group))
    wide = by_channel(mean, member[...])
    total = jnp.zeros((cols, channels), F32)
    for r in range(rows):
        away = cells[r].astype(F32) - wide
        total = total + away * away
    spread = by_group(jnp.sum(total, axis=0, keepdims=True), member[...])
    lines = lax.broadcasted_iota(jnp.int32, (8, LANES), 0)
    block = jnp.where(lines == 0, mean, jnp.where(lines == 1, spread, 0.0))
    stats[...] = block
    for out, r in ((up, 0), (down, rows - 1)):
        out[:cols, :] = cells[r].astype(F32)
        out[cols:, :] = jnp.zeros((8, channels), F32)
        out[cols : cols + 8, :LANES] = block
        out[cols + 2 : cols + 3, :cols] = mask[r].astype(F32)


def first_message_kernel(count, sizes, cells, mask, above, below, own, other, near, far, stats):
    rows, cols, channels = cells.shape
    base = stats_row(rows)
    keep = edges_kept(*sizes)
    mean, spread = merged(own[0:1], own[1:2], other[0:1], other[1:2], count)
    lines = lax.broadcasted_iota(jnp.int32, (8, LANES), 0)
    block = jnp.where(lines == 0, mean, jnp.where(lines == 1, spread, 0.0))
    stats[...] = block
    lane = lax.broadcasted_iota(jnp.int32, (rows + 2, LANES), 1)
    edges = []
    for c in (0, cols - 1):
        body = jnp.concatenate(
            [above[c : c + 1, :], cells[:, c, :].astype(F32), below[c : c + 1, :]], axis=0
        )
        holes = jnp.concatenate(
            [
                above[cols + 2 : cols + 3, c : c + 1] * keep[0],
                mask[:, 0, :].astype(F32)[:, c : c + 1],
                below[cols + 2 : cols + 3, c : c + 1] * keep[1],
            ],
            axis=0,
        )
        edges.append((body, jnp.where(lane == 0, jnp.broadcast_to(holes, lane.shape), 0.0)))
    even = even_col()
    for out, swapped in ((near, False), (far, True)):
        first, last = edges[0], edges[1]
        if swapped:
            first, last = last, first
        out[...] = jnp.zeros(out.shape, BF16)
        out[: rows + 2, :channels] = jnp.where(even, last[0], first[0]).astype(BF16)
        out[: rows + 2, channels:] = jnp.where(even, last[1], first[1]).astype(BF16)
    near[base : base + 8, :LANES] = packed(mean, spread)


def stats_row(rows):
    return -(-(rows + 2) // 16) * 16


def packed(mean, spread):
    return jnp.concatenate(
        [*thirds(mean), *thirds(spread), jnp.zeros((2, mean.shape[1]), BF16)], axis=0
    )


def unpacked(message, base):
    block = message[base : base + 16, :LANES].astype(F32)
    return block[0:1] + block[1:2] + block[2:3], block[3:4] + block[4:5] + block[5:6]


def second_message_kernel(rows, count, far, own, got, out, stats):
    base = stats_row(rows)
    mean, spread = merged(own[0:1], own[1:2], *unpacked(got, base), count)
    lines = lax.broadcasted_iota(jnp.int32, (8, LANES), 0)
    stats[...] = jnp.where(lines == 0, mean, jnp.where(lines == 1, spread, 0.0))
    out[...] = far[...]
    out[base : base + 8, :LANES] = packed(mean, spread)


def windows_kernel(
    count, depth, half_rows, sizes, stride, cells, mask, above, below, near, far, own, member,
    norm_gain, norm_shift, mask_weight, bias, weight, out, total, even, odd, kept, holes,
):
    rows, cols, channels = cells.shape
    base = stats_row(rows)
    group = 2 * cols
    mean, spread = merged(own[0:1], own[1:2], *unpacked(far, base), count)
    mean_row = by_channel(mean, member[...])
    gain_row = by_channel(lax.rsqrt(spread * (0.5 / count) + EPS), member[...]) * norm_gain[...]
    offset_row = norm_shift[...]

    def act(x):
        v = (x.astype(F32) - mean_row) * gain_row + offset_row
        return v / (1.0 + jnp.exp(-v))

    keep = edges_kept(*sizes)
    is_even = even_col()
    from_near = near[: rows + 2, :].astype(F32)
    from_far = far[: rows + 2, :].astype(F32)
    left = jnp.where(is_even, from_far, from_near)
    right = jnp.where(is_even, from_near, from_far)
    left_act = act(left[:, :channels]) * keep[2]
    right_act = act(right[:, :channels]) * keep[3]
    place = lax.broadcasted_iota(jnp.int32, (cols, channels), 0)

    tall = jnp.concatenate(
        [
            above[cols + 2 : cols + 3, :cols] * keep[0],
            mask[:, 0, :].astype(F32),
            below[cols + 2 : cols + 3, :cols] * keep[1],
        ],
        axis=0,
    )
    tall = jnp.concatenate(
        [
            left[:, channels : channels + 1] * keep[2],
            tall,
            right[:, channels : channels + 1] * keep[3],
            jnp.zeros((rows + 2, LANES - cols - 2), F32),
        ],
        axis=1,
    )
    tall = jnp.concatenate([tall, jnp.zeros((LANES - rows - 2, LANES), F32)], axis=0)
    flipped = tall.T
    moved = [flipped[dx : dx + cols, :] for dx in range(3)]
    ending = jnp.concatenate([jnp.ones((cols, 1), F32), jnp.zeros((cols, 6), F32)], axis=1)

    def hole_row(r):
        return jnp.concatenate([m[:, r : r + 3] for m in moved] + [ending], axis=1)

    def row_of(r):
        if r == 0:
            value = act(above[:cols, :])
        elif r == rows + 1:
            value = act(below[:cols, :])
        else:
            value = act(cells[r - 1])
        lo, hi = left_act[r : r + 1], right_act[r : r + 1]
        if r == 0 or r == rows + 1:
            edge = keep[0] if r == 0 else keep[1]
            value, lo, hi = value * edge, lo * edge, hi * edge
        before = jnp.where(place == 0, jnp.broadcast_to(lo, value.shape), pltpu.roll(value, 1, 0))
        behind = jnp.where(
            place == cols - 1, jnp.broadcast_to(hi, value.shape), pltpu.roll(value, cols - 1, 0)
        )
        return before, value, behind

    for pair in range(rows // 2 + 1):
        one = row_of(2 * pair)
        two = row_of(2 * pair + 1)
        for dx in range(3):
            even[dx, pair * group : (pair + 1) * group, :] = jnp.concatenate(
                [one[dx], two[dx]], axis=0
            ).astype(BF16)
            if pair:
                odd[dx, (pair - 1) * group : pair * group, :] = jnp.concatenate(
                    [kept[dx], one[dx]], axis=0
                ).astype(BF16)
            kept[dx] = two[dx]
        if pair < rows // 2:
            holes[pair * group : (pair + 1) * group, :16] = jnp.concatenate(
                [hole_row(2 * pair), hole_row(2 * pair + 1)], axis=0
            ).astype(BF16)

    def fill(step, carry):
        at = pl.multiple_of(step * group, group)
        for part in range(PARTS):
            for half in range(2):
                pieces = []
                for tap, first, width in segments(half, depth, half_rows):
                    source = odd if tap // 3 == 1 else even
                    start = at + (group if tap // 3 == 2 else 0)
                    lane = part * depth + first
                    pieces.append(source[tap % 3, pl.ds(start, group), lane : lane + width])
                out[2 * part + half, pl.ds(at, group), :] = jnp.concatenate(pieces, axis=1)
        return carry

    lax.fori_loop(0, rows // 2, fill, 0)

    taps = mask_weight[...]
    order = [3 * (k % 3) + k // 3 for k in range(TAPS)]
    table = jnp.concatenate(
        [taps[t : t + 1] for t in order] + [bias[...], jnp.zeros((6, channels), F32)], axis=0
    )
    part = lax.axis_index("dp") // stride
    spots = 2 * part, 2 * part + 1
    result = None
    for piece in thirds(table):
        term = jnp.dot(holes[:, :16], piece, preferred_element_type=F32)
        result = term if result is None else result + term
    for half in range(2):
        result = result + jnp.dot(
            out[spots[half]],
            weight[half * half_rows : (half + 1) * half_rows, :],
            preferred_element_type=F32,
        )
    total[...] = result


def next_kernel(stride, flip, lhs, one, two, three, four, total, out, held):
    cut = one.shape[0]
    owner = (lax.axis_index("dp") // stride) ^ flip
    core = lax.rem(lax.axis_index("row"), 2)
    spots = 2 * owner + core, 2 * owner + 1 - core
    for spot, (head, tail) in enumerate(((one, two), (three, four))):
        held[spot, :cut, :] = head[...]
        held[spot, cut:, :] = tail[...]
    out[...] = (
        total[...]
        + jnp.dot(lhs[spots[0]], held[0], preferred_element_type=F32)
        + jnp.dot(lhs[spots[1]], held[1], preferred_element_type=F32)
    ).astype(out.dtype)


def local(features, hole_mask, norm_gain, norm_shift, conv_weight, mask_weight, conv_bias):
    rows, cols, channels = features.shape[1:]
    cells = rows * cols
    per_group = channels // GROUPS
    n_dp, n_row, n_col = lax.axis_size("dp"), lax.axis_size("row"), lax.axis_size("col")
    if n_col != 4 or rows % 2 or cols % 8:
        raise ValueError("unsupported sizes")
    stride = n_dp // PARTS
    at_dp, at_row = lax.axis_index("dp"), lax.axis_index("row")

    shard = conv_weight
    bit = 1
    while bit < stride:
        other = swap(shard, "dp", bit)
        upper = (at_dp // bit) % 2 == 1
        shard = jnp.concatenate(
            [jnp.where(upper, other, shard), jnp.where(upper, shard, other)], axis=1
        )
        bit *= 2
    depth = shard.shape[1]
    weight = shard.reshape(TAPS * depth, channels)
    half_rows = TAPS * depth // 2
    first = -(-(half_rows // 2) // LANES) * LANES

    piece_a, piece_b = pl.pallas_call(
        cut_kernel,
        out_shape=[
            jax.ShapeDtypeStruct((first, channels), BF16),
            jax.ShapeDtypeStruct((half_rows - first, channels), BF16),
        ],
        in_specs=[HBM],
        out_specs=[VMEM, VMEM],
        scratch_shapes=[pltpu.SemaphoreType.DMA((2,))],
        compiler_params=params(4),
        name="cut",
    )(pltpu.with_memory_space_constraint(weight, pltpu.HBM))
    x_b = swap(piece_b, "dp", stride)
    y_a = swap(piece_a, "dp", 2 * stride)

    image = features[0]
    mask = hole_mask.reshape(rows, 1, cols)
    member = (
        lax.broadcasted_iota(jnp.int32, (channels, LANES), 0) // per_group
        == lax.broadcasted_iota(jnp.int32, (channels, LANES), 1)
    ).astype(BF16)
    stats_shape = jax.ShapeDtypeStruct((8, LANES), F32)
    line_shape = jax.ShapeDtypeStruct((cols + 8, channels), F32)
    up, down, stats = pl.pallas_call(
        functools.partial(stats_kernel, per_group),
        out_shape=[line_shape, line_shape, stats_shape],
        in_specs=[VMEM] * 3,
        out_specs=[VMEM] * 3,
        compiler_params=params(4),
        cost_estimate=cost(0, 4 << 20),
        name="stats",
    )(image, mask, member)
    x_a = swap(after(piece_a, stats), "dp", stride)
    y_b = swap(after(piece_b, stats), "dp", 2 * stride)
    count = float(cells * per_group)
    if n_row == 2:
        above = below = swap(jnp.where(at_row == 0, down, up), "row", 1)
        other = above[cols : cols + 8, :LANES]
    else:
        above = shift(down, "row", 1)
        below = shift(up, "row", -1)
        bit = 1
        other = swap(stats, "row", bit)
        while 2 * bit < n_row:
            mean, spread = merged(stats[0], stats[1], other[0], other[1], count)
            stats = jnp.concatenate([mean[None], spread[None], jnp.zeros((6, LANES), F32)])
            count *= 2.0
            bit *= 2
            other = swap(stats, "row", bit)

    message = jax.ShapeDtypeStruct((stats_row(rows) + 16, channels + LANES), BF16)
    near, far, stats = pl.pallas_call(
        functools.partial(first_message_kernel, count, (n_row, n_col)),
        out_shape=[message, message, stats_shape],
        in_specs=[VMEM] * 6,
        out_specs=[VMEM] * 3,
        compiler_params=params(4),
        cost_estimate=cost(0, 1 << 20),
        name="message_one",
    )(image, mask, above, below, stats, other)
    near = swap(near, "col", 1)
    count *= 2.0
    far, stats = pl.pallas_call(
        functools.partial(second_message_kernel, rows, count),
        out_shape=[message, stats_shape],
        in_specs=[VMEM] * 3,
        out_specs=[VMEM] * 2,
        compiler_params=params(4),
        cost_estimate=cost(0, 1 << 18),
        name="message_two",
    )(far, stats, near)
    far = swap(far, "col", 3)
    x_b, y_a = after(x_b, far), after(y_a, far)
    count *= 2.0
    d_a = swap(y_a, "dp", stride)
    d_b = swap(x_b, "dp", 2 * stride)

    flops = 4 * cells * half_rows * channels
    lhs, total = pl.pallas_call(
        functools.partial(windows_kernel, count, depth, half_rows, (n_row, n_col), stride),
        out_shape=[
            pltpu.VMEM((2 * PARTS, cells, half_rows), BF16),
            pltpu.VMEM((cells, channels), F32),
        ],
        in_specs=[VMEM] * 13,
        out_specs=[VMEM, VMEM],
        scratch_shapes=[
            pltpu.VMEM((3, cells + 2 * cols, channels), BF16),
            pltpu.VMEM((3, cells, channels), BF16),
            pltpu.VMEM((3, cols, channels), F32),
            pltpu.VMEM((cells, LANES), BF16),
        ],
        compiler_params=params(14),
        cost_estimate=cost(2 * flops, 24 << 20),
        name="windows",
    )(
        image, mask, above, below, near, far, stats, member,
        norm_gain[None], norm_shift[None], mask_weight, conv_bias[None], weight,
    )

    x_a, y_b = after(x_a, lhs), after(y_b, lhs)
    for number, (head, tail) in enumerate(((x_a, x_b), (y_a, y_b), (d_a, d_b))):
        last = number == 2
        total = pl.pallas_call(
            functools.partial(next_kernel, stride, number + 1),
            out_shape=jax.ShapeDtypeStruct((cells, channels), BF16)
            if last
            else pltpu.VMEM((cells, channels), F32),
            in_specs=[VMEM] * 6,
            out_specs=VMEM,
            scratch_shapes=[pltpu.VMEM((2, half_rows, channels), BF16)],
            compiler_params=params(8),
            cost_estimate=cost(flops, 4 << 20),
            name="last" if last else "next",
        )(
            lhs, head, tail,
            swap(head, "row", 1),
            swap(tail, "row", 1),
            total,
        )
    return total.reshape(1, rows, cols, channels)


def solution(mesh):
    in_specs = (
        P("dp", "row", "col", None),
        P("dp", "row", "col"),
        P(),
        P(),
        P(None, "dp", None),
        P(),
        P(),
    )
    out_specs = P("dp", "row", "col", None)
    return jax.shard_map(local, mesh=mesh, in_specs=in_specs, out_specs=out_specs, check_vma=False)
```

```python
import functools

import jax
import jax.numpy as jnp
from jax import lax
from jax.experimental import pallas as pl
from jax.experimental.pallas import tpu as pltpu
from jax.sharding import PartitionSpec as P


GROUPS = 32
EPS = 1e-05
TAPS = 9
PARTS = 4
LANES = 128


VMEM = pl.BlockSpec(memory_space=pltpu.VMEM)
HBM = pl.BlockSpec(memory_space=pltpu.HBM)
F32 = jnp.float32
BF16 = jnp.bfloat16


def swap(value, axis, bit):
    size = lax.axis_size(axis)
    return lax.ppermute(value, axis, [(i, i ^ bit) for i in range(size)])


def cross(value, bits):
    n_dp, n_row = lax.axis_size("dp"), lax.axis_size("row")
    pairs = [
        (d * n_row + r, (d ^ bits[r % 2]) * n_row + r) for d in range(n_dp) for r in range(n_row)
    ]
    return lax.ppermute(value, ("dp", "row"), pairs)


def shift(value, axis, step):
    size = lax.axis_size(axis)
    pairs = [(i, i + step) for i in range(size) if 0 <= i + step < size]
    return lax.ppermute(value, axis, pairs)


def after(value, *others):
    return lax.optimization_barrier((value, *others))[0]


def params(mib):
    return pltpu.CompilerParams(vmem_limit_bytes=mib << 20)


def cost(flops, size):
    return pl.CostEstimate(flops=flops, bytes_accessed=size, transcendentals=0)


def thirds(value):
    high = value.astype(BF16)
    rest = value - high.astype(F32)
    middle = rest.astype(BF16)
    low = (rest - middle.astype(F32)).astype(BF16)
    return high, middle, low


def exact_dot(value, ones, dims):
    total = None
    for piece in thirds(value):
        term = lax.dot_general(piece, ones, (dims, ((), ())), preferred_element_type=F32)
        total = term if total is None else total + term
    return total


def membership(channels, per_group):
    channel = lax.broadcasted_iota(jnp.int32, (channels, LANES), 0)
    low = lax.broadcasted_iota(jnp.int32, (channels, LANES), 1) * per_group
    return jnp.where((channel >= low) & (channel < low + per_group), 1.0, 0.0).astype(BF16)


def by_group(value, member):
    return exact_dot(jnp.broadcast_to(value, (16, value.shape[1])), member, ((1,), (0,)))[:1]


def by_channel(value, member):
    return exact_dot(jnp.broadcast_to(value, (16, value.shape[1])), member, ((1,), (1,)))[:1]


def merged(mean, spread, other_mean, other_spread, count):
    gap = mean - other_mean
    return (mean + other_mean) * 0.5, spread + other_spread + gap * gap * (count * 0.5)


def edges_kept(count_row, count_col):
    row, col = lax.axis_index("row"), lax.axis_index("col")
    inside = (row > 0, row < count_row - 1, col > 0, col < count_col - 1)
    return [jnp.where(flag, 1.0, 0.0).astype(F32) for flag in inside]


def even_col():
    return lax.rem(lax.axis_index("col"), 2) == 0


def spans(half, depth):
    full = depth // LANES * LANES
    taps = [half * 5 + t for t in range(TAPS // 2)]
    pieces = [(tap, 0, full) for tap in taps]
    pieces += [(tap, full, depth - full) for tap in taps]
    pieces.append((TAPS // 2, half * depth // 2, depth // 2))
    return pieces


def cut_kernel(flip, weight, *refs):
    outs, sems = refs[:-1], refs[-1]
    depth = weight.shape[1]
    for half in range(2):

        @pl.when(lax.rem(lax.axis_index("row"), 2) == half ^ flip)
        def _():
            which, at, copies = 0, 0, []
            for number, (tap, start, width) in enumerate(spans(half, depth)):
                if at == outs[which].shape[0]:
                    which, at = which + 1, 0
                copies.append(
                    pltpu.make_async_copy(
                        weight.at[tap, pl.ds(start, width)],
                        outs[which].at[pl.ds(at, width)],
                        sems.at[number],
                    )
                )
                at += width
            for copy in copies:
                copy.start()
            for copy in copies:
                copy.wait()


def regrouped(value):
    tiles = [value[:, t * LANES : (t + 1) * LANES] for t in range(5)]
    lane = lax.broadcasted_iota(jnp.int32, tiles[0].shape, 1)
    main = [tiles[0]]
    for part in range(1, PARTS):
        mixed = jnp.where(lane >= 32 * part, tiles[part], tiles[part + 1])
        main.append(pltpu.roll(mixed, LANES - 32 * part, 1))
    rest = tiles[4]
    for part in range(2, -1, -1):
        rest = jnp.where(lane < 32 * (part + 1), tiles[part + 1], rest)
    return jnp.concatenate(main + [rest], axis=1)


def stats_kernel(per_group, cells, mask, up, down, stats, holes, held, sem):
    fetch = pltpu.make_async_copy(mask, held, sem)
    fetch.start()
    rows, cols, channels = cells.shape
    count = float(rows * cols)
    member = membership(channels, per_group)
    total = jnp.zeros((cols, channels), F32)
    for r in range(rows):
        total = total + cells[r].astype(F32)
    sums = jnp.sum(total, axis=0, keepdims=True)
    mean = by_group(sums, member) * (1.0 / (count * per_group))
    wide = by_channel(mean, member)
    total = jnp.zeros((cols, channels), F32)
    for r in range(rows):
        away = cells[r].astype(F32) - wide
        total = total + away * away
    spread = by_group(jnp.sum(total, axis=0, keepdims=True), member)
    lines = lax.broadcasted_iota(jnp.int32, (8, LANES), 0)
    block = jnp.where(lines == 0, mean, jnp.where(lines == 1, spread, 0.0))
    stats[...] = block
    fetch.wait()
    marks = held[:, 0, :].astype(F32)
    holes[...] = marks
    for out, r in ((up, 0), (down, rows - 1)):
        out[:cols, :] = cells[r].astype(F32)
        out[cols:, :] = jnp.zeros((8, channels), F32)
        out[cols : cols + 8, :LANES] = block
        out[cols + 2 : cols + 3, :cols] = marks[r : r + 1, :]


def first_message_kernel(count, sizes, cells, mask, above, below, own, other, near, far, stats):
    rows, cols, channels = cells.shape
    base = stats_row(rows)
    keep = edges_kept(*sizes)
    mean, spread = merged(own[0:1], own[1:2], other[0:1], other[1:2], count)
    lines = lax.broadcasted_iota(jnp.int32, (8, LANES), 0)
    block = jnp.where(lines == 0, mean, jnp.where(lines == 1, spread, 0.0))
    stats[...] = block
    lane = lax.broadcasted_iota(jnp.int32, (rows + 2, LANES), 1)
    edges = []
    for c in (0, cols - 1):
        body = jnp.concatenate(
            [above[c : c + 1, :], cells[:, c, :].astype(F32), below[c : c + 1, :]], axis=0
        )
        holes = jnp.concatenate(
            [
                above[cols + 2 : cols + 3, c : c + 1] * keep[0],
                mask[:, c : c + 1],
                below[cols + 2 : cols + 3, c : c + 1] * keep[1],
            ],
            axis=0,
        )
        edges.append((body, jnp.where(lane == 0, jnp.broadcast_to(holes, lane.shape), 0.0)))
    even = even_col()
    for out, swapped in ((near, False), (far, True)):
        first, last = edges[0], edges[1]
        if swapped:
            first, last = last, first
        out[...] = jnp.zeros(out.shape, BF16)
        out[: rows + 2, :channels] = jnp.where(even, last[0], first[0]).astype(BF16)
        out[: rows + 2, channels:] = jnp.where(even, last[1], first[1]).astype(BF16)
    near[base : base + 8, :LANES] = packed(mean, spread)


def stats_row(rows):
    return -(-(rows + 2) // 16) * 16


def packed(mean, spread):
    return jnp.concatenate(
        [*thirds(mean), *thirds(spread), jnp.zeros((2, mean.shape[1]), BF16)], axis=0
    )


def unpacked(message, base):
    block = message[base : base + 16, :LANES].astype(F32)
    return block[0:1] + block[1:2] + block[2:3], block[3:4] + block[4:5] + block[5:6]


def second_message_kernel(rows, count, own, got, stats):
    base = stats_row(rows)
    mean, spread = merged(own[0:1], own[1:2], *unpacked(got, base), count)
    lines = lax.broadcasted_iota(jnp.int32, (8, LANES), 0)
    stats[...] = jnp.where(lines == 0, mean, jnp.where(lines == 1, spread, 0.0))


def kind_of(tap):
    return tap % 3 + (3 if tap // 3 == 1 else 0)


def windows_of(src, packs, group, part, half, low, high, begin=0, end=TAPS // 2 + 1):
    tiles = []
    for number in range(begin, end):
        tap = half * 5 + number
        if number == TAPS // 2:
            tiles.append(packs[2 * part + half, low:high, :])
        else:
            move = group if tap // 3 == 2 else 0
            tiles.append(src[kind_of(tap), part, low + move : high + move, :])
    return jnp.concatenate(tiles, axis=1)


def windows_kernel(
    count, depth, half_rows, sizes, stride, cells, mask, above, below, near, far, own, other, norm_gain, norm_shift, mask_weight, bias, weight, src, packs, total, rests, kept, holes, held,
):
    rows, cols, channels = cells.shape
    group = 2 * cols
    member = membership(channels, channels // GROUPS)
    mean, spread = merged(own[0:1], own[1:2], other[0:1], other[1:2], count)
    mean_row = by_channel(mean, member)
    gain_row = by_channel(lax.rsqrt(spread * (0.5 / count) + EPS), member) * norm_gain[...]
    offset_row = norm_shift[...]

    def act(x):
        v = (x.astype(F32) - mean_row) * gain_row + offset_row
        half = 0.5 * v
        return half + half * jnp.tanh(half)

    keep = edges_kept(*sizes)
    is_even = even_col()
    from_near = near[: rows + 2, :].astype(F32)
    from_far = far[: rows + 2, :].astype(F32)
    left = jnp.where(is_even, from_far, from_near)
    right = jnp.where(is_even, from_near, from_far)
    left_act = regrouped(act(left[:, :channels]) * keep[2])
    right_act = regrouped(act(right[:, :channels]) * keep[3])
    place = lax.broadcasted_iota(jnp.int32, (cols, channels), 0)

    tall = jnp.concatenate(
        [
            above[cols + 2 : cols + 3, :cols] * keep[0],
            mask[...],
            below[cols + 2 : cols + 3, :cols] * keep[1],
        ],
        axis=0,
    )
    tall = jnp.concatenate(
        [
            left[:, channels : channels + 1] * keep[2],
            tall,
            right[:, channels : channels + 1] * keep[3],
            jnp.zeros((rows + 2, LANES - cols - 2), F32),
        ],
        axis=1,
    )
    tall = jnp.concatenate([tall, jnp.zeros((LANES - rows - 2, LANES), F32)], axis=0)
    flipped = tall.T
    moved = [flipped[dx : dx + cols, :] for dx in range(3)]
    ones = jnp.ones((cols, 1), F32)

    def hole_row(r):
        once = jnp.concatenate([m[:, r : r + 3] for m in moved] + [ones], axis=1)
        return jnp.concatenate([once, once, once, jnp.zeros((cols, 2), F32)], axis=1)

    def row_of(r):
        if r == 0:
            value = act(above[:cols, :])
        elif r == rows + 1:
            value = act(below[:cols, :])
        else:
            value = act(cells[r - 1])
        value = regrouped(value)
        lo, hi = left_act[r : r + 1], right_act[r : r + 1]
        if r == 0 or r == rows + 1:
            edge = keep[0] if r == 0 else keep[1]
            value, lo, hi = value * edge, lo * edge, hi * edge
        before = jnp.where(place == 0, jnp.broadcast_to(lo, value.shape), pltpu.roll(value, 1, 0))
        behind = jnp.where(
            place == cols - 1, jnp.broadcast_to(hi, value.shape), pltpu.roll(value, cols - 1, 0)
        )
        return before, value, behind

    def put(kind, place, first, second):
        value = jnp.concatenate([first, second], axis=0).astype(BF16)
        low, high = place * group, (place + 1) * group
        for part in range(PARTS):
            src[kind, part, low:high, :] = value[:, part * LANES : (part + 1) * LANES]
        rests[kind, low:high, :] = value[:, PARTS * LANES :]

    for pair in range(rows // 2 + 1):
        one = row_of(2 * pair)
        two = row_of(2 * pair + 1)
        for dx in range(3):
            put(dx, pair, one[dx], two[dx])
            if pair:
                put(3 + dx, pair - 1, kept[dx], one[dx])
            kept[dx] = two[dx]
        if pair < rows // 2:
            holes[pair * group : (pair + 1) * group, :32] = jnp.concatenate(
                [hole_row(2 * pair), hole_row(2 * pair + 1)], axis=0
            ).astype(BF16)

    def fill(step, carry):
        at = pl.multiple_of(step * group, group)
        lane = lax.broadcasted_iota(jnp.int32, (group, LANES), 1)

        def rest_of(tap):
            start = at + (group if tap // 3 == 2 else 0)
            return rests[kind_of(tap), pl.ds(start, group), :]

        def turned(value, amount):
            return pltpu.roll(value, amount % LANES, 1) if amount % LANES else value

        for half in range(2):
            taps = [half * 5 + t for t in range(4)]
            ends = [rest_of(tap) for tap in taps]
            for part in range(PARTS):
                spot = 2 * part + half
                rest = turned(ends[3], 32 * (3 - part))
                for number in (2, 1, 0):
                    piece = turned(ends[number], 32 * (number - part))
                    rest = jnp.where(lane < 32 * (number + 1), piece, rest)
                packs[spot, pl.ds(at, group), :LANES] = rest
                final = src[4, part, pl.ds(at, group), :]
                if half:
                    extra = turned(rest_of(4), 48 - 32 * part)
                    final = jnp.where(lane < 48, turned(final, 48), extra)
                packs[spot, pl.ds(at, group), LANES:] = final[:, : half_rows - 5 * LANES]
        return carry

    lax.fori_loop(0, rows // 2, fill, 0)

    taps = mask_weight[...]
    order = [3 * (k % 3) + k // 3 for k in range(TAPS)]
    table = jnp.concatenate([taps[t : t + 1] for t in order] + [bias[...]], axis=0)
    table = jnp.concatenate([*thirds(table), jnp.zeros((2, channels), BF16)], axis=0)
    part = lax.axis_index("dp") // stride
    result = jnp.dot(holes[:, :32], table, preferred_element_type=F32)
    for half in range(2):
        at = 0
        for tap, start, width in spans(half, depth):
            held[half, at : at + width, :] = weight[tap, start : start + width, :]
            at += width
    for half in range(2):
        lhs = windows_of(src, packs, group, part, half, 0, rows * cols)
        result = result + jnp.dot(lhs, held[half], preferred_element_type=F32)
    total[...] = result


def next_kernel(stride, group, src, packs, one, two, three, four, total, out, held):
    cut = one.shape[0]
    part = lax.axis_index("dp") // stride
    core = lax.rem(lax.axis_index("row"), 2)
    for spot, head, tail in ((core, one, two), (1 - core, three, four)):
        held[spot, :cut, :] = head[...]
        held[spot, cut:, :] = tail[...]
    result = total[...]
    for half in range(2):
        lhs = windows_of(src, packs, group, part ^ (1 + half), half, 0, total.shape[0])
        result = result + jnp.dot(lhs, held[half], preferred_element_type=F32)
    out[...] = result


def head_kernel(stride, group, flip, src, packs, direct, passed, total, out, held):
    owner = (lax.axis_index("dp") // stride) ^ flip
    core = lax.rem(lax.axis_index("row"), 2)
    held[core] = direct[...]
    held[1 - core] = passed[...]
    end = direct.shape[0] // LANES
    result = total[...]
    for half in range(2):
        lhs = windows_of(src, packs, group, owner, half, 0, total.shape[0], 0, end)
        result = result + jnp.dot(lhs, held[half], preferred_element_type=F32)
    out[...] = result


def piece_kernel(stride, group, flips, side, begin, src, packs, piece, total, out):
    part = lax.axis_index("dp") // stride
    for half in range(2):

        @pl.when(lax.rem(lax.axis_index("row"), 2) == half ^ side)
        def _():
            owner = part ^ flips[half]
            lhs = windows_of(src, packs, group, owner, half, 0, total.shape[0], begin)
            out[...] = total[...] + jnp.dot(lhs, piece[...], preferred_element_type=F32)


def last_kernel(stride, group, flip, begin, src, packs, piece, total, out, done, sems):
    cells = total.shape[0]
    owner = (lax.axis_index("dp") // stride) ^ flip
    bounds = [0, 320, 560, 720, cells] if cells == 800 else [0, cells]
    for half in range(2):

        @pl.when(lax.rem(lax.axis_index("row"), 2) != half)
        def _():
            copies = []
            for number, (low, high) in enumerate(zip(bounds[:-1], bounds[1:])):
                lhs = windows_of(src, packs, group, owner, half, low, high, begin)
                done[low:high, :] = (
                    total[low:high, :] + jnp.dot(lhs, piece[...], preferred_element_type=F32)
                ).astype(BF16)
                copies.append(
                    pltpu.make_async_copy(
                        done.at[pl.ds(low, high - low)],
                        out.at[pl.ds(low, high - low)],
                        sems.at[number],
                    )
                )
                copies[-1].start()
            for copy in copies:
                copy.wait()


def local(features, hole_mask, norm_gain, norm_shift, conv_weight, mask_weight, conv_bias):
    rows, cols, channels = features.shape[1:]
    cells = rows * cols
    per_group = channels // GROUPS
    n_dp, n_row, n_col = lax.axis_size("dp"), lax.axis_size("row"), lax.axis_size("col")
    if n_col != 4 or rows % 2 or cols % 8 or channels != 5 * LANES:
        raise ValueError("unsupported sizes")
    stride = n_dp // PARTS
    at_dp, at_row = lax.axis_index("dp"), lax.axis_index("row")

    shard = conv_weight
    bit = 1
    while bit < stride:
        other = swap(shard, "dp", bit)
        upper = (at_dp // bit) % 2 == 1
        shard = jnp.concatenate(
            [jnp.where(upper, other, shard), jnp.where(upper, shard, other)], axis=1
        )
        bit *= 2
    depth = shard.shape[1]
    half_rows = TAPS * depth // 2
    first = -(-(half_rows // 2) // LANES) * LANES

    source = pltpu.with_memory_space_constraint(shard, pltpu.HBM)

    def cut(flip, sizes):
        return pl.pallas_call(
            functools.partial(cut_kernel, flip),
            out_shape=[pltpu.VMEM((size, channels), BF16) for size in sizes],
            in_specs=[HBM],
            out_specs=[VMEM] * len(sizes),
            scratch_shapes=[pltpu.SemaphoreType.DMA((TAPS,))],
            compiler_params=params(4),
            cost_estimate=cost(0, 2 << 20),
            name="cut",
        )(source)

    straight, turned = (stride, 2 * stride), (2 * stride, stride)
    piece_a, piece_b = cut(0, (first, half_rows - first))
    w_a = cross(piece_a, straight)
    w_b = cross(piece_b, straight)
    (piece_c,) = cut(1, (half_rows,))

    image = features[0]
    mask = hole_mask.reshape(rows, 1, cols)
    stats_shape = jax.ShapeDtypeStruct((8, LANES), F32)
    line_shape = jax.ShapeDtypeStruct((cols + 8, channels), F32)
    up, down, stats, holes = pl.pallas_call(
        functools.partial(stats_kernel, per_group),
        out_shape=[line_shape, line_shape, stats_shape, pltpu.VMEM((rows, cols), F32)],
        in_specs=[VMEM, HBM],
        out_specs=[VMEM] * 4,
        scratch_shapes=[pltpu.VMEM((rows, 1, cols), jnp.int32), pltpu.SemaphoreType.DMA],
        compiler_params=params(4),
        cost_estimate=cost(0, 4 << 20),
        name="stats",
    )(image, pltpu.with_memory_space_constraint(mask, pltpu.HBM))
    count = float(cells * per_group)
    if n_row == 2:
        above = below = swap(jnp.where(at_row == 0, down, up), "row", 1)
        other = above[cols : cols + 8, :LANES]
    else:
        above = shift(down, "row", 1)
        below = shift(up, "row", -1)
        bit = 1
        other = swap(stats, "row", bit)
        while 2 * bit < n_row:
            mean, spread = merged(stats[0], stats[1], other[0], other[1], count)
            stats = jnp.concatenate([mean[None], spread[None], jnp.zeros((6, LANES), F32)])
            count *= 2.0
            bit *= 2
            other = swap(stats, "row", bit)

    message = jax.ShapeDtypeStruct((stats_row(rows) + 16, channels + LANES), BF16)
    near, far, stats = pl.pallas_call(
        functools.partial(first_message_kernel, count, (n_row, n_col)),
        out_shape=[message, message, stats_shape],
        in_specs=[VMEM] * 6,
        out_specs=[VMEM] * 3,
        compiler_params=params(4),
        cost_estimate=cost(0, 1 << 20),
        name="message_one",
    )(image, holes, above, below, stats, other)
    w_c = cross(after(piece_c, near), straight)
    near = swap(near, "col", 1)
    far = lax.ppermute(far, "col", [(1, 2), (2, 1)])
    count *= 2.0
    stats = pl.pallas_call(
        functools.partial(second_message_kernel, rows, count),
        out_shape=stats_shape,
        in_specs=[VMEM] * 2,
        out_specs=VMEM,
        compiler_params=params(4),
        cost_estimate=cost(0, 1 << 18),
        name="message_two",
    )(stats, near)
    other = swap(stats, "col", 2)
    w_a, w_b = after(w_a, stats), after(w_b, stats)
    d_a = cross(w_a, turned)
    f_a, f_b = swap(w_a, "row", 1), swap(w_b, "row", 1)
    count *= 2.0

    flops = 4 * cells * half_rows * channels
    src, packs, total = pl.pallas_call(
        functools.partial(windows_kernel, count, depth, half_rows, (n_row, n_col), stride),
        out_shape=[
            pltpu.VMEM((6, PARTS, cells + 2 * cols, LANES), BF16),
            pltpu.VMEM((2 * PARTS, cells, half_rows - PARTS * LANES), BF16),
            pltpu.VMEM((cells, channels), F32),
        ],
        in_specs=[VMEM] * 13,
        out_specs=[VMEM] * 3,
        scratch_shapes=[
            pltpu.VMEM((6, cells + 2 * cols, LANES), BF16),
            pltpu.VMEM((3, cols, channels), F32),
            pltpu.VMEM((cells, LANES), BF16),
            pltpu.VMEM((2, half_rows, channels), BF16),
        ],
        compiler_params=params(14),
        cost_estimate=cost(2 * flops, 24 << 20),
        name="windows",
    )(
        image, holes, above, below, near, far, stats, other,
        norm_gain[None], norm_shift[None], mask_weight, conv_bias[None], shard,
    )

    d_b = cross(after(w_b, src), turned)
    f_c = swap(after(w_c, src), "row", 1)
    accumulated = pltpu.VMEM((cells, channels), F32)
    total = pl.pallas_call(
        functools.partial(next_kernel, stride, 2 * cols),
        out_shape=accumulated,
        in_specs=[VMEM] * 7,
        out_specs=VMEM,
        scratch_shapes=[pltpu.VMEM((2, half_rows, channels), BF16)],
        compiler_params=params(8),
        cost_estimate=cost(flops, 4 << 20),
        name="next",
    )(src, packs, w_a, w_b, f_a, f_b, total)

    def piece_call(flips, side, begin, piece, total):
        return pl.pallas_call(
            functools.partial(piece_kernel, stride, 2 * cols, flips, side, begin),
            out_shape=accumulated,
            in_specs=[VMEM] * 4,
            out_specs=VMEM,
            compiler_params=params(8),
            cost_estimate=cost(flops // 2, 4 << 20),
            name="piece",
        )(src, packs, piece, total)

    d_a = after(d_a, total)
    total = pl.pallas_call(
        functools.partial(head_kernel, stride, 2 * cols, 3),
        out_shape=accumulated,
        in_specs=[VMEM] * 5,
        out_specs=VMEM,
        scratch_shapes=[pltpu.VMEM((2, first, channels), BF16)],
        compiler_params=params(8),
        cost_estimate=cost(flops // 2, 4 << 20),
        name="head",
    )(src, packs, d_a, swap(d_a, "row", 1), total)
    total = piece_call((2, 1), 1, 0, w_c, total)
    total = piece_call((2, 1), 0, 0, f_c, total)
    total = piece_call((3, 3), 0, first // LANES, d_b, total)
    total = pl.pallas_call(
        functools.partial(last_kernel, stride, 2 * cols, 3, first // LANES),
        out_shape=jax.ShapeDtypeStruct((cells, channels), BF16),
        in_specs=[VMEM] * 4,
        out_specs=HBM,
        scratch_shapes=[
            pltpu.VMEM((cells, channels), BF16),
            pltpu.SemaphoreType.DMA((4,)),
        ],
        compiler_params=params(8),
        cost_estimate=cost(flops // 4, 4 << 20),
        name="last",
    )(src, packs, swap(d_b, "row", 1), total)
    return total.reshape(1, rows, cols, channels)


def solution(mesh):
    in_specs = (
        P("dp", "row", "col", None),
        P("dp", "row", "col"),
        P(),
        P(),
        P(None, "dp", None),
        P(),
        P(),
    )
    out_specs = P("dp", "row", "col", None)
    return jax.shard_map(local, mesh=mesh, in_specs=in_specs, out_specs=out_specs, check_vma=False)
```

```python
import functools

import jax
import jax.numpy as jnp
from jax import lax
from jax.experimental import pallas as pl
from jax.experimental.pallas import tpu as pltpu
from jax.sharding import PartitionSpec as P


GROUPS = 32
EPS = 1e-05
TAPS = 9
PARTS = 4
LANES = 128


VMEM = pl.BlockSpec(memory_space=pltpu.VMEM)
HBM = pl.BlockSpec(memory_space=pltpu.HBM)
F32 = jnp.float32
BF16 = jnp.bfloat16


def swap(value, axis, bit):
    size = lax.axis_size(axis)
    return lax.ppermute(value, axis, [(i, i ^ bit) for i in range(size)])


def cross(value, bits):
    n_dp, n_row = lax.axis_size("dp"), lax.axis_size("row")
    pairs = [
        (d * n_row + r, (d ^ bits[r % 2]) * n_row + r) for d in range(n_dp) for r in range(n_row)
    ]
    return lax.ppermute(value, ("dp", "row"), pairs)


def shift(value, axis, step):
    size = lax.axis_size(axis)
    pairs = [(i, i + step) for i in range(size) if 0 <= i + step < size]
    return lax.ppermute(value, axis, pairs)


def after(value, *others):
    return lax.optimization_barrier((value, *others))[0]


def params(mib):
    return pltpu.CompilerParams(vmem_limit_bytes=mib << 20)


def cost(flops, size):
    return pl.CostEstimate(flops=flops, bytes_accessed=size, transcendentals=0)


def thirds(value):
    high = value.astype(BF16)
    rest = value - high.astype(F32)
    middle = rest.astype(BF16)
    low = (rest - middle.astype(F32)).astype(BF16)
    return high, middle, low


def exact_dot(value, ones, dims):
    total = None
    for piece in thirds(value):
        term = lax.dot_general(piece, ones, (dims, ((), ())), preferred_element_type=F32)
        total = term if total is None else total + term
    return total


def membership(channels, per_group):
    channel = lax.broadcasted_iota(jnp.int32, (channels, LANES), 0)
    low = lax.broadcasted_iota(jnp.int32, (channels, LANES), 1) * per_group
    return jnp.where((channel >= low) & (channel < low + per_group), 1.0, 0.0).astype(BF16)


def by_group(value, member):
    return exact_dot(jnp.broadcast_to(value, (16, value.shape[1])), member, ((1,), (0,)))[:1]


def by_channel(value, member):
    return exact_dot(jnp.broadcast_to(value, (16, value.shape[1])), member, ((1,), (1,)))[:1]


def merged(mean, spread, other_mean, other_spread, count):
    gap = mean - other_mean
    return (mean + other_mean) * 0.5, spread + other_spread + gap * gap * (count * 0.5)


def edges_kept(count_row, count_col):
    row, col = lax.axis_index("row"), lax.axis_index("col")
    inside = (row > 0, row < count_row - 1, col > 0, col < count_col - 1)
    return [jnp.where(flag, 1.0, 0.0).astype(F32) for flag in inside]


def even_col():
    return lax.rem(lax.axis_index("col"), 2) == 0


def spans(half, depth):
    full = depth // LANES * LANES
    taps = [half * 5 + t for t in range(TAPS // 2)]
    pieces = [(tap, 0, full) for tap in taps]
    pieces += [(tap, full, depth - full) for tap in taps]
    pieces.append((TAPS // 2, half * depth // 2, depth // 2))
    return pieces


def cut_kernel(flip, weight, *refs):
    outs, sems = refs[:-1], refs[-1]
    depth = weight.shape[1]
    for half in range(2):

        @pl.when(lax.rem(lax.axis_index("row"), 2) == half ^ flip)
        def _():
            which, at, copies = 0, 0, []
            for number, (tap, start, width) in enumerate(spans(half, depth)):
                if at == outs[which].shape[0]:
                    which, at = which + 1, 0
                copies.append(
                    pltpu.make_async_copy(
                        weight.at[tap, pl.ds(start, width)],
                        outs[which].at[pl.ds(at, width)],
                        sems.at[number],
                    )
                )
                at += width
            for copy in copies:
                copy.start()
            for copy in copies:
                copy.wait()


def regrouped(value):
    tiles = [value[:, t * LANES : (t + 1) * LANES] for t in range(5)]
    lane = lax.broadcasted_iota(jnp.int32, tiles[0].shape, 1)
    main = [tiles[0]]
    for part in range(1, PARTS):
        mixed = jnp.where(lane >= 32 * part, tiles[part], tiles[part + 1])
        main.append(pltpu.roll(mixed, LANES - 32 * part, 1))
    rest = tiles[4]
    for part in range(2, -1, -1):
        rest = jnp.where(lane < 32 * (part + 1), tiles[part + 1], rest)
    return jnp.concatenate(main + [rest], axis=1)


def stats_kernel(per_group, cells, mask, up, down, stats, holes, held, sem):
    fetch = pltpu.make_async_copy(mask, held, sem)
    fetch.start()
    rows, cols, channels = cells.shape
    count = float(rows * cols)
    member = membership(channels, per_group)
    total = jnp.zeros((cols, channels), F32)
    for r in range(rows):
        total = total + cells[r].astype(F32)
    sums = jnp.sum(total, axis=0, keepdims=True)
    mean = by_group(sums, member) * (1.0 / (count * per_group))
    wide = by_channel(mean, member)
    total = jnp.zeros((cols, channels), F32)
    for r in range(rows):
        away = cells[r].astype(F32) - wide
        total = total + away * away
    spread = by_group(jnp.sum(total, axis=0, keepdims=True), member)
    lines = lax.broadcasted_iota(jnp.int32, (8, LANES), 0)
    block = jnp.where(lines == 0, mean, jnp.where(lines == 1, spread, 0.0))
    stats[...] = block
    fetch.wait()
    marks = held[:, 0, :].astype(F32)
    holes[...] = marks
    for out, r in ((up, 0), (down, rows - 1)):
        out[:cols, :] = cells[r].astype(F32)
        out[cols:, :] = jnp.zeros((8, channels), F32)
        out[cols : cols + 8, :LANES] = block
        out[cols + 2 : cols + 3, :cols] = marks[r : r + 1, :]


def first_message_kernel(count, sizes, cells, mask, above, below, own, other, near, far, stats):
    rows, cols, channels = cells.shape
    base = stats_row(rows)
    keep = edges_kept(*sizes)
    mean, spread = merged(own[0:1], own[1:2], other[0:1], other[1:2], count)
    lines = lax.broadcasted_iota(jnp.int32, (8, LANES), 0)
    block = jnp.where(lines == 0, mean, jnp.where(lines == 1, spread, 0.0))
    stats[...] = block
    lane = lax.broadcasted_iota(jnp.int32, (rows + 2, LANES), 1)
    edges = []
    for c in (0, cols - 1):
        body = jnp.concatenate(
            [above[c : c + 1, :], cells[:, c, :].astype(F32), below[c : c + 1, :]], axis=0
        )
        holes = jnp.concatenate(
            [
                above[cols + 2 : cols + 3, c : c + 1] * keep[0],
                mask[:, c : c + 1],
                below[cols + 2 : cols + 3, c : c + 1] * keep[1],
            ],
            axis=0,
        )
        edges.append((body, jnp.where(lane == 0, jnp.broadcast_to(holes, lane.shape), 0.0)))
    even = even_col()
    for out, swapped in ((near, False), (far, True)):
        first, last = edges[0], edges[1]
        if swapped:
            first, last = last, first
        out[...] = jnp.zeros(out.shape, BF16)
        out[: rows + 2, :channels] = jnp.where(even, last[0], first[0]).astype(BF16)
        out[: rows + 2, channels:] = jnp.where(even, last[1], first[1]).astype(BF16)
    near[base : base + 8, :LANES] = packed(mean, spread)


def stats_row(rows):
    return -(-(rows + 2) // 16) * 16


def packed(mean, spread):
    return jnp.concatenate(
        [*thirds(mean), *thirds(spread), jnp.zeros((2, mean.shape[1]), BF16)], axis=0
    )


def unpacked(message, base):
    block = message[base : base + 16, :LANES].astype(F32)
    return block[0:1] + block[1:2] + block[2:3], block[3:4] + block[4:5] + block[5:6]


def second_message_kernel(rows, count, own, got, stats):
    base = stats_row(rows)
    mean, spread = merged(own[0:1], own[1:2], *unpacked(got, base), count)
    lines = lax.broadcasted_iota(jnp.int32, (8, LANES), 0)
    stats[...] = jnp.where(lines == 0, mean, jnp.where(lines == 1, spread, 0.0))


def kind_of(tap):
    return tap % 3 + (3 if tap // 3 == 1 else 0)


def windows_of(src, packs, group, part, half, low, high, begin=0, end=TAPS // 2 + 1):
    tiles = []
    for number in range(begin, end):
        tap = half * 5 + number
        if number == TAPS // 2:
            tiles.append(packs[2 * part + half, low:high, :])
        else:
            move = group if tap // 3 == 2 else 0
            tiles.append(src[kind_of(tap), part, low + move : high + move, :])
    return jnp.concatenate(tiles, axis=1)


def windows_kernel(
    count, depth, half_rows, sizes, stride, cells, mask, above, below, near, far, own, other, norm_gain, norm_shift, mask_weight, bias, weight, src, packs, total, rests, kept, holes, held,
):
    rows, cols, channels = cells.shape
    group = 2 * cols
    member = membership(channels, channels // GROUPS)
    mean, spread = merged(own[0:1], own[1:2], other[0:1], other[1:2], count)
    mean_row = by_channel(mean, member)
    gain_row = by_channel(lax.rsqrt(spread * (0.5 / count) + EPS), member) * norm_gain[...]
    offset_row = norm_shift[...]

    def act(x):
        v = (x.astype(F32) - mean_row) * gain_row + offset_row
        half = 0.5 * v
        return half + half * jnp.tanh(half)

    keep = edges_kept(*sizes)
    is_even = even_col()
    from_near = near[: rows + 2, :].astype(F32)
    from_far = far[: rows + 2, :].astype(F32)
    left = jnp.where(is_even, from_far, from_near)
    right = jnp.where(is_even, from_near, from_far)
    left_act = regrouped(act(left[:, :channels]) * keep[2])
    right_act = regrouped(act(right[:, :channels]) * keep[3])
    place = lax.broadcasted_iota(jnp.int32, (cols, channels), 0)

    tall = jnp.concatenate(
        [
            above[cols + 2 : cols + 3, :cols] * keep[0],
            mask[...],
            below[cols + 2 : cols + 3, :cols] * keep[1],
        ],
        axis=0,
    )
    tall = jnp.concatenate(
        [
            left[:, channels : channels + 1] * keep[2],
            tall,
            right[:, channels : channels + 1] * keep[3],
            jnp.zeros((rows + 2, LANES - cols - 2), F32),
        ],
        axis=1,
    )
    tall = jnp.concatenate([tall, jnp.zeros((LANES - rows - 2, LANES), F32)], axis=0)
    flipped = tall.T
    moved = [flipped[dx : dx + cols, :] for dx in range(3)]
    ones = jnp.ones((cols, 1), F32)

    def hole_row(r):
        once = jnp.concatenate([m[:, r : r + 3] for m in moved] + [ones], axis=1)
        return jnp.concatenate([once, once, once, jnp.zeros((cols, 2), F32)], axis=1)

    def row_of(r):
        if r == 0:
            value = act(above[:cols, :])
        elif r == rows + 1:
            value = act(below[:cols, :])
        else:
            value = act(cells[r - 1])
        value = regrouped(value)
        lo, hi = left_act[r : r + 1], right_act[r : r + 1]
        if r == 0 or r == rows + 1:
            edge = keep[0] if r == 0 else keep[1]
            value, lo, hi = value * edge, lo * edge, hi * edge
        before = jnp.where(place == 0, jnp.broadcast_to(lo, value.shape), pltpu.roll(value, 1, 0))
        behind = jnp.where(
            place == cols - 1, jnp.broadcast_to(hi, value.shape), pltpu.roll(value, cols - 1, 0)
        )
        return before, value, behind

    def put(kind, place, first, second):
        value = jnp.concatenate([first, second], axis=0).astype(BF16)
        low, high = place * group, (place + 1) * group
        for part in range(PARTS):
            src[kind, part, low:high, :] = value[:, part * LANES : (part + 1) * LANES]
        rests[kind, low:high, :] = value[:, PARTS * LANES :]

    for pair in range(rows // 2 + 1):
        one = row_of(2 * pair)
        two = row_of(2 * pair + 1)
        for dx in range(3):
            put(dx, pair, one[dx], two[dx])
            if pair:
                put(3 + dx, pair - 1, kept[dx], one[dx])
            kept[dx] = two[dx]
        if pair < rows // 2:
            holes[pair * group : (pair + 1) * group, :32] = jnp.concatenate(
                [hole_row(2 * pair), hole_row(2 * pair + 1)], axis=0
            ).astype(BF16)

    def fill(step, carry):
        at = pl.multiple_of(step * group, group)
        lane = lax.broadcasted_iota(jnp.int32, (group, LANES), 1)

        def rest_of(tap):
            start = at + (group if tap // 3 == 2 else 0)
            return rests[kind_of(tap), pl.ds(start, group), :]

        def turned(value, amount):
            return pltpu.roll(value, amount % LANES, 1) if amount % LANES else value

        for half in range(2):
            taps = [half * 5 + t for t in range(4)]
            ends = [rest_of(tap) for tap in taps]
            shifted = []
            for amount in range(4):
                mixed = ends[(3 + amount) % 4]
                for part in (2, 1, 0):
                    mixed = jnp.where(lane < 32 * (part + 1), ends[(part + amount) % 4], mixed)
                shifted.append(turned(mixed, 32 * amount))
            for part in range(PARTS):
                spot = 2 * part + half
                rest = shifted[(3 - part) % 4]
                for number in (2, 1, 0):
                    rest = jnp.where(lane < 32 * (number + 1), shifted[(number - part) % 4], rest)
                packs[spot, pl.ds(at, group), :LANES] = rest
                final = src[4, part, pl.ds(at, group), :]
                if half:
                    extra = turned(rest_of(4), 48 - 32 * part)
                    final = jnp.where(lane < 48, turned(final, 48), extra)
                packs[spot, pl.ds(at, group), LANES:] = final[:, : half_rows - 5 * LANES]
        return carry

    lax.fori_loop(0, rows // 2, fill, 0)

    taps = mask_weight[...]
    order = [3 * (k % 3) + k // 3 for k in range(TAPS)]
    table = jnp.concatenate([taps[t : t + 1] for t in order] + [bias[...]], axis=0)
    table = jnp.concatenate([*thirds(table), jnp.zeros((2, channels), BF16)], axis=0)
    part = lax.axis_index("dp") // stride
    result = jnp.dot(holes[:, :32], table, preferred_element_type=F32)
    for half in range(2):
        at = 0
        for tap, start, width in spans(half, depth):
            held[half, at : at + width, :] = weight[tap, start : start + width, :]
            at += width
    for half in range(2):
        lhs = windows_of(src, packs, group, part, half, 0, rows * cols)
        result = result + jnp.dot(lhs, held[half], preferred_element_type=F32)
    total[...] = result


def next_kernel(stride, group, src, packs, one, two, three, four, total, out, held):
    cut = one.shape[0]
    part = lax.axis_index("dp") // stride
    core = lax.rem(lax.axis_index("row"), 2)
    for spot, head, tail in ((core, one, two), (1 - core, three, four)):
        held[spot, :cut, :] = head[...]
        held[spot, cut:, :] = tail[...]
    result = total[...]
    for half in range(2):
        lhs = windows_of(src, packs, group, part ^ (1 + half), half, 0, total.shape[0])
        result = result + jnp.dot(lhs, held[half], preferred_element_type=F32)
    out[...] = result


def head_kernel(stride, group, flip, src, packs, direct, passed, total, out, held):
    owner = (lax.axis_index("dp") // stride) ^ flip
    core = lax.rem(lax.axis_index("row"), 2)
    held[core] = direct[...]
    held[1 - core] = passed[...]
    end = direct.shape[0] // LANES
    result = total[...]
    for half in range(2):
        lhs = windows_of(src, packs, group, owner, half, 0, total.shape[0], 0, end)
        result = result + jnp.dot(lhs, held[half], preferred_element_type=F32)
    out[...] = result


def piece_kernel(stride, group, flips, side, begin, src, packs, piece, total, out):
    part = lax.axis_index("dp") // stride
    for half in range(2):

        @pl.when(lax.rem(lax.axis_index("row"), 2) == half ^ side)
        def _():
            owner = part ^ flips[half]
            lhs = windows_of(src, packs, group, owner, half, 0, total.shape[0], begin)
            out[...] = total[...] + jnp.dot(lhs, piece[...], preferred_element_type=F32)


def last_kernel(stride, group, flip, begin, src, packs, piece, total, out, done, sems):
    cells = total.shape[0]
    owner = (lax.axis_index("dp") // stride) ^ flip
    bounds = [0, 320, 560, 720, cells] if cells == 800 else [0, cells]
    for half in range(2):

        @pl.when(lax.rem(lax.axis_index("row"), 2) != half)
        def _():
            copies = []
            for number, (low, high) in enumerate(zip(bounds[:-1], bounds[1:])):
                lhs = windows_of(src, packs, group, owner, half, low, high, begin)
                done[low:high, :] = (
                    total[low:high, :] + jnp.dot(lhs, piece[...], preferred_element_type=F32)
                ).astype(BF16)
                copies.append(
                    pltpu.make_async_copy(
                        done.at[pl.ds(low, high - low)],
                        out.at[pl.ds(low, high - low)],
                        sems.at[number],
                    )
                )
                copies[-1].start()
            for copy in copies:
                copy.wait()


def local(features, hole_mask, norm_gain, norm_shift, conv_weight, mask_weight, conv_bias):
    rows, cols, channels = features.shape[1:]
    cells = rows * cols
    per_group = channels // GROUPS
    n_dp, n_row, n_col = lax.axis_size("dp"), lax.axis_size("row"), lax.axis_size("col")
    if n_col != 4 or rows % 2 or cols % 8 or channels != 5 * LANES:
        raise ValueError("unsupported sizes")
    stride = n_dp // PARTS
    at_dp, at_row = lax.axis_index("dp"), lax.axis_index("row")

    shard = conv_weight
    bit = 1
    while bit < stride:
        other = swap(shard, "dp", bit)
        upper = (at_dp // bit) % 2 == 1
        shard = jnp.concatenate(
            [jnp.where(upper, other, shard), jnp.where(upper, shard, other)], axis=1
        )
        bit *= 2
    depth = shard.shape[1]
    half_rows = TAPS * depth // 2
    first = -(-(half_rows // 2) // LANES) * LANES

    source = pltpu.with_memory_space_constraint(shard, pltpu.HBM)

    def cut(flip, sizes):
        return pl.pallas_call(
            functools.partial(cut_kernel, flip),
            out_shape=[pltpu.VMEM((size, channels), BF16) for size in sizes],
            in_specs=[HBM],
            out_specs=[VMEM] * len(sizes),
            scratch_shapes=[pltpu.SemaphoreType.DMA((TAPS,))],
            compiler_params=params(4),
            cost_estimate=cost(0, 2 << 20),
            name="cut",
        )(source)

    straight, turned = (stride, 2 * stride), (2 * stride, stride)
    piece_a, piece_b = cut(0, (first, half_rows - first))
    w_a = cross(piece_a, straight)
    w_b = cross(piece_b, straight)
    (piece_c,) = cut(1, (half_rows,))

    image = features[0]
    mask = hole_mask.reshape(rows, 1, cols)
    stats_shape = jax.ShapeDtypeStruct((8, LANES), F32)
    line_shape = jax.ShapeDtypeStruct((cols + 8, channels), F32)
    up, down, stats, holes = pl.pallas_call(
        functools.partial(stats_kernel, per_group),
        out_shape=[line_shape, line_shape, stats_shape, pltpu.VMEM((rows, cols), F32)],
        in_specs=[VMEM, HBM],
        out_specs=[VMEM] * 4,
        scratch_shapes=[pltpu.VMEM((rows, 1, cols), jnp.int32), pltpu.SemaphoreType.DMA],
        compiler_params=params(4),
        cost_estimate=cost(0, 4 << 20),
        name="stats",
    )(image, pltpu.with_memory_space_constraint(mask, pltpu.HBM))
    count = float(cells * per_group)
    if n_row == 2:
        above = below = swap(jnp.where(at_row == 0, down, up), "row", 1)
        other = above[cols : cols + 8, :LANES]
    else:
        above = shift(down, "row", 1)
        below = shift(up, "row", -1)
        bit = 1
        other = swap(stats, "row", bit)
        while 2 * bit < n_row:
            mean, spread = merged(stats[0], stats[1], other[0], other[1], count)
            stats = jnp.concatenate([mean[None], spread[None], jnp.zeros((6, LANES), F32)])
            count *= 2.0
            bit *= 2
            other = swap(stats, "row", bit)

    message = jax.ShapeDtypeStruct((stats_row(rows) + 16, channels + LANES), BF16)
    near, far, stats = pl.pallas_call(
        functools.partial(first_message_kernel, count, (n_row, n_col)),
        out_shape=[message, message, stats_shape],
        in_specs=[VMEM] * 6,
        out_specs=[VMEM] * 3,
        compiler_params=params(4),
        cost_estimate=cost(0, 1 << 20),
        name="message_one",
    )(image, holes, above, below, stats, other)
    w_c = cross(after(piece_c, near), straight)
    near = swap(near, "col", 1)
    far = lax.ppermute(far, "col", [(1, 2), (2, 1)])
    count *= 2.0
    stats = pl.pallas_call(
        functools.partial(second_message_kernel, rows, count),
        out_shape=stats_shape,
        in_specs=[VMEM] * 2,
        out_specs=VMEM,
        compiler_params=params(4),
        cost_estimate=cost(0, 1 << 18),
        name="message_two",
    )(stats, near)
    other = swap(stats, "col", 2)
    w_a, w_b = after(w_a, stats), after(w_b, stats)
    d_a = cross(w_a, turned)
    f_a, f_b = swap(w_a, "row", 1), swap(w_b, "row", 1)
    count *= 2.0

    flops = 4 * cells * half_rows * channels
    src, packs, total = pl.pallas_call(
        functools.partial(windows_kernel, count, depth, half_rows, (n_row, n_col), stride),
        out_shape=[
            pltpu.VMEM((6, PARTS, cells + 2 * cols, LANES), BF16),
            pltpu.VMEM((2 * PARTS, cells, half_rows - PARTS * LANES), BF16),
            pltpu.VMEM((cells, channels), F32),
        ],
        in_specs=[VMEM] * 13,
        out_specs=[VMEM] * 3,
        scratch_shapes=[
            pltpu.VMEM((6, cells + 2 * cols, LANES), BF16),
            pltpu.VMEM((3, cols, channels), F32),
            pltpu.VMEM((cells, LANES), BF16),
            pltpu.VMEM((2, half_rows, channels), BF16),
        ],
        compiler_params=params(14),
        cost_estimate=cost(2 * flops, 24 << 20),
        name="windows",
    )(
        image, holes, above, below, near, far, stats, other,
        norm_gain[None], norm_shift[None], mask_weight, conv_bias[None], shard,
    )

    d_b = cross(after(w_b, src), turned)
    f_c = swap(after(w_c, src), "row", 1)
    accumulated = pltpu.VMEM((cells, channels), F32)
    total = pl.pallas_call(
        functools.partial(next_kernel, stride, 2 * cols),
        out_shape=accumulated,
        in_specs=[VMEM] * 7,
        out_specs=VMEM,
        scratch_shapes=[pltpu.VMEM((2, half_rows, channels), BF16)],
        compiler_params=params(8),
        cost_estimate=cost(flops, 4 << 20),
        name="next",
    )(src, packs, w_a, w_b, f_a, f_b, total)

    def piece_call(flips, side, begin, piece, total):
        return pl.pallas_call(
            functools.partial(piece_kernel, stride, 2 * cols, flips, side, begin),
            out_shape=accumulated,
            in_specs=[VMEM] * 4,
            out_specs=VMEM,
            compiler_params=params(8),
            cost_estimate=cost(flops // 2, 4 << 20),
            name="piece",
        )(src, packs, piece, total)

    d_a = after(d_a, total)
    total = pl.pallas_call(
        functools.partial(head_kernel, stride, 2 * cols, 3),
        out_shape=accumulated,
        in_specs=[VMEM] * 5,
        out_specs=VMEM,
        scratch_shapes=[pltpu.VMEM((2, first, channels), BF16)],
        compiler_params=params(8),
        cost_estimate=cost(flops // 2, 4 << 20),
        name="head",
    )(src, packs, d_a, swap(d_a, "row", 1), total)
    total = piece_call((2, 1), 1, 0, w_c, total)
    total = piece_call((3, 3), 0, first // LANES, d_b, total)
    total = piece_call((2, 1), 0, 0, f_c, total)
    total = pl.pallas_call(
        functools.partial(last_kernel, stride, 2 * cols, 3, first // LANES),
        out_shape=jax.ShapeDtypeStruct((cells, channels), BF16),
        in_specs=[VMEM] * 4,
        out_specs=HBM,
        scratch_shapes=[
            pltpu.VMEM((cells, channels), BF16),
            pltpu.SemaphoreType.DMA((4,)),
        ],
        compiler_params=params(8),
        cost_estimate=cost(flops // 4, 4 << 20),
        name="last",
    )(src, packs, swap(d_b, "row", 1), total)
    return total.reshape(1, rows, cols, channels)


def solution(mesh):
    in_specs = (
        P("dp", "row", "col", None),
        P("dp", "row", "col"),
        P(),
        P(),
        P(None, "dp", None),
        P(),
        P(),
    )
    out_specs = P("dp", "row", "col", None)
    return jax.shard_map(local, mesh=mesh, in_specs=in_specs, out_specs=out_specs, check_vma=False)
```

```python
import functools

import jax
import jax.numpy as jnp
from jax import lax
from jax.experimental import pallas as pl
from jax.experimental.pallas import tpu as pltpu
from jax.sharding import PartitionSpec as P


GROUPS = 32
EPS = 1e-05
TAPS = 9
PARTS = 4
LANES = 128


VMEM = pl.BlockSpec(memory_space=pltpu.VMEM)
HBM = pl.BlockSpec(memory_space=pltpu.HBM)
F32 = jnp.float32
BF16 = jnp.bfloat16


def swap(value, axis, bit):
    size = lax.axis_size(axis)
    return lax.ppermute(value, axis, [(i, i ^ bit) for i in range(size)])


def cross(value, bits):
    n_dp, n_row = lax.axis_size("dp"), lax.axis_size("row")
    pairs = [
        (d * n_row + r, (d ^ bits[r % 2]) * n_row + r) for d in range(n_dp) for r in range(n_row)
    ]
    return lax.ppermute(value, ("dp", "row"), pairs)


def shift(value, axis, step):
    size = lax.axis_size(axis)
    pairs = [(i, i + step) for i in range(size) if 0 <= i + step < size]
    return lax.ppermute(value, axis, pairs)


def after(value, *others):
    return lax.optimization_barrier((value, *others))[0]


def params(mib):
    return pltpu.CompilerParams(vmem_limit_bytes=mib << 20)


def cost(flops, size):
    return pl.CostEstimate(flops=flops, bytes_accessed=size, transcendentals=0)


def thirds(value):
    high = value.astype(BF16)
    rest = value - high.astype(F32)
    middle = rest.astype(BF16)
    low = (rest - middle.astype(F32)).astype(BF16)
    return high, middle, low


def exact_dot(value, ones, dims):
    total = None
    for piece in thirds(value):
        term = lax.dot_general(piece, ones, (dims, ((), ())), preferred_element_type=F32)
        total = term if total is None else total + term
    return total


def membership(channels, per_group):
    channel = lax.broadcasted_iota(jnp.int32, (channels, LANES), 0)
    low = lax.broadcasted_iota(jnp.int32, (channels, LANES), 1) * per_group
    return jnp.where((channel >= low) & (channel < low + per_group), 1.0, 0.0).astype(BF16)


def by_group(value, member):
    return exact_dot(jnp.broadcast_to(value, (16, value.shape[1])), member, ((1,), (0,)))[:1]


def by_channel(value, member):
    return exact_dot(jnp.broadcast_to(value, (16, value.shape[1])), member, ((1,), (1,)))[:1]


def merged(mean, spread, other_mean, other_spread, count):
    gap = mean - other_mean
    return (mean + other_mean) * 0.5, spread + other_spread + gap * gap * (count * 0.5)


def edges_kept(count_row, count_col):
    row, col = lax.axis_index("row"), lax.axis_index("col")
    inside = (row > 0, row < count_row - 1, col > 0, col < count_col - 1)
    return [jnp.where(flag, 1.0, 0.0).astype(F32) for flag in inside]


def even_col():
    return lax.rem(lax.axis_index("col"), 2) == 0


def spans(half, depth):
    full = depth // LANES * LANES
    taps = [half * 5 + t for t in range(TAPS // 2)]
    pieces = [(tap, 0, full) for tap in taps]
    pieces += [(tap, full, depth - full) for tap in taps]
    pieces.append((TAPS // 2, half * depth // 2, depth // 2))
    return pieces


def cut_kernel(flip, weight, *refs):
    outs, sems = refs[:-1], refs[-1]
    depth = weight.shape[1]
    for half in range(2):

        @pl.when(lax.rem(lax.axis_index("row"), 2) == half ^ flip)
        def _():
            which, at, copies = 0, 0, []
            for number, (tap, start, width) in enumerate(spans(half, depth)):
                if at == outs[which].shape[0]:
                    which, at = which + 1, 0
                copies.append(
                    pltpu.make_async_copy(
                        weight.at[tap, pl.ds(start, width)],
                        outs[which].at[pl.ds(at, width)],
                        sems.at[number],
                    )
                )
                at += width
            for copy in copies:
                copy.start()
            for copy in copies:
                copy.wait()


def regrouped(value):
    tiles = [value[:, t * LANES : (t + 1) * LANES] for t in range(5)]
    lane = lax.broadcasted_iota(jnp.int32, tiles[0].shape, 1)
    main = [tiles[0]]
    for part in range(1, PARTS):
        mixed = jnp.where(lane >= 32 * part, tiles[part], tiles[part + 1])
        main.append(pltpu.roll(mixed, LANES - 32 * part, 1))
    rest = tiles[4]
    for part in range(2, -1, -1):
        rest = jnp.where(lane < 32 * (part + 1), tiles[part + 1], rest)
    return jnp.concatenate(main + [rest], axis=1)


def stats_kernel(per_group, cells, mask, up, down, stats, holes, held, sem):
    fetch = pltpu.make_async_copy(mask, held, sem)
    fetch.start()
    rows, cols, channels = cells.shape
    count = float(rows * cols)
    member = membership(channels, per_group)
    total = jnp.zeros((cols, channels), F32)
    for r in range(rows):
        total = total + cells[r].astype(F32)
    sums = jnp.sum(total, axis=0, keepdims=True)
    mean = by_group(sums, member) * (1.0 / (count * per_group))
    wide = by_channel(mean, member)
    total = jnp.zeros((cols, channels), F32)
    for r in range(rows):
        away = cells[r].astype(F32) - wide
        total = total + away * away
    spread = by_group(jnp.sum(total, axis=0, keepdims=True), member)
    lines = lax.broadcasted_iota(jnp.int32, (8, LANES), 0)
    block = jnp.where(lines == 0, mean, jnp.where(lines == 1, spread, 0.0))
    stats[...] = block
    fetch.wait()
    marks = held[:, 0, :].astype(F32)
    holes[...] = marks
    for out, r in ((up, 0), (down, rows - 1)):
        out[:cols, :] = cells[r].astype(F32)
        out[cols:, :] = jnp.zeros((8, channels), F32)
        out[cols : cols + 8, :LANES] = block
        out[cols + 2 : cols + 3, :cols] = marks[r : r + 1, :]


def first_message_kernel(count, sizes, cells, mask, above, below, own, other, near, far, stats):
    rows, cols, channels = cells.shape
    base = stats_row(rows)
    keep = edges_kept(*sizes)
    mean, spread = merged(own[0:1], own[1:2], other[0:1], other[1:2], count)
    lines = lax.broadcasted_iota(jnp.int32, (8, LANES), 0)
    block = jnp.where(lines == 0, mean, jnp.where(lines == 1, spread, 0.0))
    stats[...] = block
    lane = lax.broadcasted_iota(jnp.int32, (rows + 2, LANES), 1)
    edges = []
    for c in (0, cols - 1):
        body = jnp.concatenate(
            [above[c : c + 1, :], cells[:, c, :].astype(F32), below[c : c + 1, :]], axis=0
        )
        holes = jnp.concatenate(
            [
                above[cols + 2 : cols + 3, c : c + 1] * keep[0],
                mask[:, c : c + 1],
                below[cols + 2 : cols + 3, c : c + 1] * keep[1],
            ],
            axis=0,
        )
        edges.append((body, jnp.where(lane == 0, jnp.broadcast_to(holes, lane.shape), 0.0)))
    even = even_col()
    for out, swapped in ((near, False), (far, True)):
        first, last = edges[0], edges[1]
        if swapped:
            first, last = last, first
        out[...] = jnp.zeros(out.shape, BF16)
        out[: rows + 2, :channels] = jnp.where(even, last[0], first[0]).astype(BF16)
        out[: rows + 2, channels:] = jnp.where(even, last[1], first[1]).astype(BF16)
    near[base : base + 8, :LANES] = packed(mean, spread)


def stats_row(rows):
    return -(-(rows + 2) // 16) * 16


def packed(mean, spread):
    return jnp.concatenate(
        [*thirds(mean), *thirds(spread), jnp.zeros((2, mean.shape[1]), BF16)], axis=0
    )


def unpacked(message, base):
    block = message[base : base + 16, :LANES].astype(F32)
    return block[0:1] + block[1:2] + block[2:3], block[3:4] + block[4:5] + block[5:6]


def second_message_kernel(rows, count, own, got, stats):
    base = stats_row(rows)
    mean, spread = merged(own[0:1], own[1:2], *unpacked(got, base), count)
    lines = lax.broadcasted_iota(jnp.int32, (8, LANES), 0)
    stats[...] = jnp.where(lines == 0, mean, jnp.where(lines == 1, spread, 0.0))


def kind_of(tap):
    return tap % 3 + (3 if tap // 3 == 1 else 0)


def windows_of(src, packs, group, part, half, low, high, begin=0, end=TAPS // 2 + 1):
    tiles = []
    for number in range(begin, end):
        tap = half * 5 + number
        if number == TAPS // 2:
            tiles.append(packs[2 * part + half, low:high, :])
        else:
            move = group if tap // 3 == 2 else 0
            tiles.append(src[kind_of(tap), part, low + move : high + move, :])
    return jnp.concatenate(tiles, axis=1)


def windows_kernel(
    count, depth, half_rows, sizes, stride, cells, mask, above, below, near, far, own, other, norm_gain, norm_shift, mask_weight, bias, weight, src, packs, total, rests, kept, holes, held,
):
    rows, cols, channels = cells.shape
    group = 2 * cols
    member = membership(channels, channels // GROUPS)
    mean, spread = merged(own[0:1], own[1:2], other[0:1], other[1:2], count)
    mean_row = by_channel(mean, member)
    gain_row = by_channel(lax.rsqrt(spread * (0.5 / count) + EPS), member) * norm_gain[...]
    offset_row = norm_shift[...]

    def act(x):
        v = (x.astype(F32) - mean_row) * gain_row + offset_row
        half = 0.5 * v
        return half + half * jnp.tanh(half)

    keep = edges_kept(*sizes)
    is_even = even_col()
    from_near = near[: rows + 2, :].astype(F32)
    from_far = far[: rows + 2, :].astype(F32)
    left = jnp.where(is_even, from_far, from_near)
    right = jnp.where(is_even, from_near, from_far)
    left_act = regrouped(act(left[:, :channels]) * keep[2])
    right_act = regrouped(act(right[:, :channels]) * keep[3])
    place = lax.broadcasted_iota(jnp.int32, (cols, channels), 0)

    tall = jnp.concatenate(
        [
            above[cols + 2 : cols + 3, :cols] * keep[0],
            mask[...],
            below[cols + 2 : cols + 3, :cols] * keep[1],
        ],
        axis=0,
    )
    tall = jnp.concatenate(
        [
            left[:, channels : channels + 1] * keep[2],
            tall,
            right[:, channels : channels + 1] * keep[3],
            jnp.zeros((rows + 2, LANES - cols - 2), F32),
        ],
        axis=1,
    )
    tall = jnp.concatenate([tall, jnp.zeros((LANES - rows - 2, LANES), F32)], axis=0)
    flipped = tall.T
    moved = [flipped[dx : dx + cols, :] for dx in range(3)]
    ones = jnp.ones((cols, 1), F32)

    def hole_row(r):
        once = jnp.concatenate([m[:, r : r + 3] for m in moved] + [ones], axis=1)
        return jnp.concatenate([once, once, once, jnp.zeros((cols, 2), F32)], axis=1)

    def row_of(r):
        if r == 0:
            value = act(above[:cols, :])
        elif r == rows + 1:
            value = act(below[:cols, :])
        else:
            value = act(cells[r - 1])
        value = regrouped(value)
        lo, hi = left_act[r : r + 1], right_act[r : r + 1]
        if r == 0 or r == rows + 1:
            edge = keep[0] if r == 0 else keep[1]
            value, lo, hi = value * edge, lo * edge, hi * edge
        before = jnp.where(place == 0, jnp.broadcast_to(lo, value.shape), pltpu.roll(value, 1, 0))
        behind = jnp.where(
            place == cols - 1, jnp.broadcast_to(hi, value.shape), pltpu.roll(value, cols - 1, 0)
        )
        return before, value, behind

    def put(kind, place, first, second):
        value = jnp.concatenate([first, second], axis=0).astype(BF16)
        low, high = place * group, (place + 1) * group
        for part in range(PARTS):
            src[kind, part, low:high, :] = value[:, part * LANES : (part + 1) * LANES]
        rests[kind, low:high, :] = value[:, PARTS * LANES :]

    for pair in range(rows // 2 + 1):
        one = row_of(2 * pair)
        two = row_of(2 * pair + 1)
        for dx in range(3):
            put(dx, pair, one[dx], two[dx])
            if pair:
                put(3 + dx, pair - 1, kept[dx], one[dx])
            kept[dx] = two[dx]
        if pair < rows // 2:
            holes[pair * group : (pair + 1) * group, :32] = jnp.concatenate(
                [hole_row(2 * pair), hole_row(2 * pair + 1)], axis=0
            ).astype(BF16)

    def fill(step, carry):
        at = pl.multiple_of(step * group, group)
        lane = lax.broadcasted_iota(jnp.int32, (group, LANES), 1)

        def rest_of(tap):
            start = at + (group if tap // 3 == 2 else 0)
            return rests[kind_of(tap), pl.ds(start, group), :]

        def turned(value, amount):
            return pltpu.roll(value, amount % LANES, 1) if amount % LANES else value

        for half in range(2):
            taps = [half * 5 + t for t in range(4)]
            ends = [rest_of(tap) for tap in taps]
            shifted = []
            for amount in range(4):
                mixed = ends[(3 + amount) % 4]
                for part in (2, 1, 0):
                    mixed = jnp.where(lane < 32 * (part + 1), ends[(part + amount) % 4], mixed)
                shifted.append(turned(mixed, 32 * amount))
            for part in range(PARTS):
                spot = 2 * part + half
                rest = shifted[(3 - part) % 4]
                for number in (2, 1, 0):
                    rest = jnp.where(lane < 32 * (number + 1), shifted[(number - part) % 4], rest)
                packs[spot, pl.ds(at, group), :LANES] = rest
                final = src[4, part, pl.ds(at, group), :]
                if half:
                    extra = turned(rest_of(4), 48 - 32 * part)
                    final = jnp.where(lane < 48, turned(final, 48), extra)
                packs[spot, pl.ds(at, group), LANES:] = final[:, : half_rows - 5 * LANES]
        return carry

    lax.fori_loop(0, rows // 2, fill, 0)

    taps = mask_weight[...]
    order = [3 * (k % 3) + k // 3 for k in range(TAPS)]
    table = jnp.concatenate([taps[t : t + 1] for t in order] + [bias[...]], axis=0)
    table = jnp.concatenate([*thirds(table), jnp.zeros((2, channels), BF16)], axis=0)
    part = lax.axis_index("dp") // stride
    result = jnp.dot(holes[:, :32], table, preferred_element_type=F32)
    for half in range(2):
        at = 0
        for tap, start, width in spans(half, depth):
            held[half, at : at + width, :] = weight[tap, start : start + width, :]
            at += width
    for half in range(2):
        lhs = windows_of(src, packs, group, part, half, 0, rows * cols)
        result = result + jnp.dot(lhs, held[half], preferred_element_type=F32)
    total[...] = result


def next_kernel(stride, group, src, packs, one, two, three, four, total, out, held):
    cut = one.shape[0]
    part = lax.axis_index("dp") // stride
    core = lax.rem(lax.axis_index("row"), 2)
    for spot, head, tail in ((core, one, two), (1 - core, three, four)):
        held[spot, :cut, :] = head[...]
        held[spot, cut:, :] = tail[...]
    result = total[...]
    for half in range(2):
        lhs = windows_of(src, packs, group, part ^ (1 + half), half, 0, total.shape[0])
        result = result + jnp.dot(lhs, held[half], preferred_element_type=F32)
    out[...] = result


def piece_kernel(stride, group, flips, side, begin, end, src, packs, piece, total, out):
    part = lax.axis_index("dp") // stride
    for half in range(2):

        @pl.when(lax.rem(lax.axis_index("row"), 2) == half ^ side)
        def _():
            owner = part ^ flips[half]
            lhs = windows_of(src, packs, group, owner, half, 0, total.shape[0], begin, end)
            out[...] = total[...] + jnp.dot(lhs, piece[...], preferred_element_type=F32)


def last_kernel(stride, group, flip, begin, src, packs, piece, total, out, done, sems):
    cells = total.shape[0]
    owner = (lax.axis_index("dp") // stride) ^ flip
    bounds = [0, 320, 560, 720, cells] if cells == 800 else [0, cells]
    for half in range(2):

        @pl.when(lax.rem(lax.axis_index("row"), 2) != half)
        def _():
            copies = []
            for number, (low, high) in enumerate(zip(bounds[:-1], bounds[1:])):
                lhs = windows_of(src, packs, group, owner, half, low, high, begin)
                done[low:high, :] = (
                    total[low:high, :] + jnp.dot(lhs, piece[...], preferred_element_type=F32)
                ).astype(BF16)
                copies.append(
                    pltpu.make_async_copy(
                        done.at[pl.ds(low, high - low)],
                        out.at[pl.ds(low, high - low)],
                        sems.at[number],
                    )
                )
                copies[-1].start()
            for copy in copies:
                copy.wait()


def local(features, hole_mask, norm_gain, norm_shift, conv_weight, mask_weight, conv_bias):
    rows, cols, channels = features.shape[1:]
    cells = rows * cols
    per_group = channels // GROUPS
    n_dp, n_row, n_col = lax.axis_size("dp"), lax.axis_size("row"), lax.axis_size("col")
    if n_col != 4 or rows % 2 or cols % 8 or channels != 5 * LANES:
        raise ValueError("unsupported sizes")
    stride = n_dp // PARTS
    at_dp, at_row = lax.axis_index("dp"), lax.axis_index("row")

    shard = conv_weight
    bit = 1
    while bit < stride:
        other = swap(shard, "dp", bit)
        upper = (at_dp // bit) % 2 == 1
        shard = jnp.concatenate(
            [jnp.where(upper, other, shard), jnp.where(upper, shard, other)], axis=1
        )
        bit *= 2
    depth = shard.shape[1]
    half_rows = TAPS * depth // 2
    first = -(-(half_rows // 2) // LANES) * LANES

    source = pltpu.with_memory_space_constraint(shard, pltpu.HBM)

    def cut(flip, sizes):
        return pl.pallas_call(
            functools.partial(cut_kernel, flip),
            out_shape=[pltpu.VMEM((size, channels), BF16) for size in sizes],
            in_specs=[HBM],
            out_specs=[VMEM] * len(sizes),
            scratch_shapes=[pltpu.SemaphoreType.DMA((TAPS,))],
            compiler_params=params(4),
            cost_estimate=cost(0, 2 << 20),
            name="cut",
        )(source)

    straight, turned = (stride, 2 * stride), (2 * stride, stride)
    piece_a, piece_b = cut(0, (first, half_rows - first))
    w_a = cross(piece_a, straight)
    w_b = cross(piece_b, straight)
    (piece_c,) = cut(1, (half_rows,))

    image = features[0]
    mask = hole_mask.reshape(rows, 1, cols)
    stats_shape = jax.ShapeDtypeStruct((8, LANES), F32)
    line_shape = jax.ShapeDtypeStruct((cols + 8, channels), F32)
    up, down, stats, holes = pl.pallas_call(
        functools.partial(stats_kernel, per_group),
        out_shape=[line_shape, line_shape, stats_shape, pltpu.VMEM((rows, cols), F32)],
        in_specs=[VMEM, HBM],
        out_specs=[VMEM] * 4,
        scratch_shapes=[pltpu.VMEM((rows, 1, cols), jnp.int32), pltpu.SemaphoreType.DMA],
        compiler_params=params(4),
        cost_estimate=cost(0, 4 << 20),
        name="stats",
    )(image, pltpu.with_memory_space_constraint(mask, pltpu.HBM))
    count = float(cells * per_group)
    if n_row == 2:
        above = below = swap(jnp.where(at_row == 0, down, up), "row", 1)
        other = above[cols : cols + 8, :LANES]
    else:
        above = shift(down, "row", 1)
        below = shift(up, "row", -1)
        bit = 1
        other = swap(stats, "row", bit)
        while 2 * bit < n_row:
            mean, spread = merged(stats[0], stats[1], other[0], other[1], count)
            stats = jnp.concatenate([mean[None], spread[None], jnp.zeros((6, LANES), F32)])
            count *= 2.0
            bit *= 2
            other = swap(stats, "row", bit)

    message = jax.ShapeDtypeStruct((stats_row(rows) + 16, channels + LANES), BF16)
    near, far, stats = pl.pallas_call(
        functools.partial(first_message_kernel, count, (n_row, n_col)),
        out_shape=[message, message, stats_shape],
        in_specs=[VMEM] * 6,
        out_specs=[VMEM] * 3,
        compiler_params=params(4),
        cost_estimate=cost(0, 1 << 20),
        name="message_one",
    )(image, holes, above, below, stats, other)
    w_c = cross(after(piece_c, near), straight)
    near = swap(near, "col", 1)
    far = lax.ppermute(far, "col", [(1, 2), (2, 1)])
    count *= 2.0
    stats = pl.pallas_call(
        functools.partial(second_message_kernel, rows, count),
        out_shape=stats_shape,
        in_specs=[VMEM] * 2,
        out_specs=VMEM,
        compiler_params=params(4),
        cost_estimate=cost(0, 1 << 18),
        name="message_two",
    )(stats, near)
    other = swap(stats, "col", 2)
    w_a, w_b = after(w_a, stats), after(w_b, stats)
    d_a = cross(w_a, turned)
    f_a, f_b = swap(w_a, "row", 1), swap(w_b, "row", 1)
    count *= 2.0

    flops = 4 * cells * half_rows * channels
    src, packs, total = pl.pallas_call(
        functools.partial(windows_kernel, count, depth, half_rows, (n_row, n_col), stride),
        out_shape=[
            pltpu.VMEM((6, PARTS, cells + 2 * cols, LANES), BF16),
            pltpu.VMEM((2 * PARTS, cells, half_rows - PARTS * LANES), BF16),
            pltpu.VMEM((cells, channels), F32),
        ],
        in_specs=[VMEM] * 13,
        out_specs=[VMEM] * 3,
        scratch_shapes=[
            pltpu.VMEM((6, cells + 2 * cols, LANES), BF16),
            pltpu.VMEM((3, cols, channels), F32),
            pltpu.VMEM((cells, LANES), BF16),
            pltpu.VMEM((2, half_rows, channels), BF16),
        ],
        compiler_params=params(14),
        cost_estimate=cost(2 * flops, 24 << 20),
        name="windows",
    )(
        image, holes, above, below, near, far, stats, other,
        norm_gain[None], norm_shift[None], mask_weight, conv_bias[None], shard,
    )

    d_b = cross(after(w_b, src), turned)
    f_c = swap(after(w_c, src), "row", 1)
    accumulated = pltpu.VMEM((cells, channels), F32)
    total = pl.pallas_call(
        functools.partial(next_kernel, stride, 2 * cols),
        out_shape=accumulated,
        in_specs=[VMEM] * 7,
        out_specs=VMEM,
        scratch_shapes=[pltpu.VMEM((2, half_rows, channels), BF16)],
        compiler_params=params(8),
        cost_estimate=cost(flops, 4 << 20),
        name="next",
    )(src, packs, w_a, w_b, f_a, f_b, total)

    def piece_call(flips, side, begin, piece, total, end=TAPS // 2 + 1):
        return pl.pallas_call(
            functools.partial(piece_kernel, stride, 2 * cols, flips, side, begin, end),
            out_shape=accumulated,
            in_specs=[VMEM] * 4,
            out_specs=VMEM,
            compiler_params=params(8),
            cost_estimate=cost(flops // 2, 4 << 20),
            name="piece",
        )(src, packs, piece, total)

    d_a = after(d_a, total)
    passed = swap(d_a, "row", 1)
    total = piece_call((3, 3), 0, 0, d_a, total, first // LANES)
    total = piece_call((3, 3), 1, 0, passed, total, first // LANES)
    total = piece_call((2, 1), 1, 0, w_c, total)
    total = piece_call((3, 3), 0, first // LANES, d_b, total)
    total = piece_call((2, 1), 0, 0, f_c, total)
    total = pl.pallas_call(
        functools.partial(last_kernel, stride, 2 * cols, 3, first // LANES),
        out_shape=jax.ShapeDtypeStruct((cells, channels), BF16),
        in_specs=[VMEM] * 4,
        out_specs=HBM,
        scratch_shapes=[
            pltpu.VMEM((cells, channels), BF16),
            pltpu.SemaphoreType.DMA((4,)),
        ],
        compiler_params=params(8),
        cost_estimate=cost(flops // 4, 4 << 20),
        name="last",
    )(src, packs, swap(d_b, "row", 1), total)
    return total.reshape(1, rows, cols, channels)


def solution(mesh):
    in_specs = (
        P("dp", "row", "col", None),
        P("dp", "row", "col"),
        P(),
        P(),
        P(None, "dp", None),
        P(),
        P(),
    )
    out_specs = P("dp", "row", "col", None)
    return jax.shard_map(local, mesh=mesh, in_specs=in_specs, out_specs=out_specs, check_vma=False)
```
